32 devices in a mesh: dp: 2 (over core), ctx: 8 (over z, x), mp: 2 (over y).
Axes of the slice: x: 2, y: 2, z: 4, core: 2. Of those that a mesh axis runs over, the one named last changes fastest.
Arguments:
- inputs: float32 [2, 1024, 896], P('dp', 'ctx'), may hold values from -6 to 6
- positions: int32 [2, 1024], P('dp'), may hold values from 0 to 1023, as said below
- attn_gain: bfloat16 [1, 896], P(None, ('dp', 'ctx')), may hold values from 0.5 to 1.5
- qkv_weight: bfloat16 [1, 896, 1152], P(None, ('dp', 'ctx'), 'mp'), may hold values from -0.1875 to 0.1875
- qkv_bias: bfloat16 [1, 2, 576], P(None, 'mp', ('dp', 'ctx')), may hold values from -5 to 5
- out_weight: bfloat16 [1, 896, 896], P(None, 'mp', ('dp', 'ctx')), may hold values from -0.75 to 0.75
- ffn_gain: bfloat16 [1, 896], P(None, ('dp', 'ctx')), may hold values from 0.5 to 1.5
- gate_up_weight: bfloat16 [1, 896, 2, 4864], P(None, ('dp', 'ctx'), None, 'mp'), may hold values from -0.1875 to 0.1875
- down_weight: bfloat16 [1, 4864, 896], P(None, 'mp', ('dp', 'ctx')), may hold values from -0.078125 to 0.078125
- cotangent: float32 [2, 1024, 896], P('dp', 'ctx'), may hold values from -6 to 6
Outputs:
- output: float32 [2, 1024, 896], P('dp', 'ctx')
- input_grad: float32 [2, 1024, 896], P('dp', 'ctx')
- attn_gain_grad: float32 [1, 896], P(None, ('dp', 'ctx'))
- qkv_weight_grad: float32 [1, 896, 1152], P(None, ('dp', 'ctx'), 'mp')
- qkv_bias_grad: float32 [1, 2, 576], P(None, 'mp', ('dp', 'ctx'))
- out_weight_grad: float32 [1, 896, 896], P(None, 'mp', ('dp', 'ctx'))
- ffn_gain_grad: float32 [1, 896], P(None, ('dp', 'ctx'))
- gate_up_grad: float32 [1, 896, 2, 4864], P(None, ('dp', 'ctx'), None, 'mp')
- down_grad: float32 [1, 4864, 896], P(None, 'mp', ('dp', 'ctx'))
The draws below stay inside these ranges and needn't reach their ends.
Inputs may be any that keep to these rules, and one draw needn't show every extreme that they name: In each sequence every position 0 to 1023 occurs once; the tokens come in blocks of 64 consecutive positions starting at multiples of 64, and the two blocks of one index of ctx are blocks c and 15 - c of the sequence for some c that depends on the index, in either order.
All inputs are finite; a program needn't handle non-finite values.
Results may differ from the reference program's by a relative error of at most 0.02.
The reference program's roundings to bfloat16 on the way count: a program that leaves them out, or rounds other values in their place, can miss the bound.
Values may be sent and summed in bfloat16 or wider, within the bound.
No kernel may reach another device: no remote copies, remote signals or barrier semaphores. Data moves between devices by JAX's collectives and lax.ppermute only.
A program may use at most 128 MiB of HBM per device.

```python
import jax
import jax.numpy as jnp
from jax import lax

D = 896
HEADS = 14
KV_HEADS = 2
HEAD_DIM = 64
FF = 4864
LAYERS = 1
GROUP = 7
BLK = 64
BLOCKS = 16
SEQ = 1024
BATCH = 2


def draw_positions(key, part):
    sequences = []
    for seq_idx in range(BATCH):
        seq_key = jax.random.fold_in(key, seq_idx + 11)
        order = jax.random.permutation(jax.random.fold_in(seq_key, 1), BLOCKS // 2).astype(jnp.int32)
        flips = jax.random.randint(jax.random.fold_in(seq_key, 2), (BLOCKS // 2,), 0, 2).astype(jnp.int32)
        first = jnp.where(flips == 0, order, BLOCKS - 1 - order)
        second = BLOCKS - 1 - first
        block_ids = jnp.stack([first, second], axis=1)
        offsets = jnp.arange(BLK, dtype=jnp.int32)
        block_locations = block_ids[:, :, None] * BLK + offsets[None, None, :]
        sequences.append(block_locations.reshape(SEQ).astype(jnp.int32))
    return jnp.stack(sequences)


def draw_qkv_bias(key, part):
    noise = jax.random.normal(jax.random.fold_in(key, 5), (LAYERS, KV_HEADS, (GROUP + 2) * HEAD_DIM), jnp.float32) * 0.5
    return jnp.clip(noise, -5.0, 5.0).astype(jnp.bfloat16)


def block_levels(own_key, shape, pieces, least, top_value):
    gain = 1.0
    for dim, blocks in pieces:
        draws = jax.random.uniform(jax.random.fold_in(jax.random.fold_in(own_key, 6), dim), (blocks,), jnp.float32, least / len(pieces), top_value / len(pieces))
        gain = gain * jnp.repeat(jnp.exp(draws), shape[dim] // blocks).reshape((-1,) + (1,) * (len(shape) - 1 - dim))
    return gain


def scatter_about(key, extent, width, bound, pieces=(), held_as=jnp.bfloat16):
    drawn = width * jax.random.normal(key, extent, jnp.float32)
    if pieces:
        drawn = drawn * block_levels(key, extent, pieces, -0.22, 0.18)
    return jnp.clip(drawn, -bound, bound).astype(held_as)


def setup_inputs(seed: int = 0) -> dict:
    key_of = jax.random.split(jax.random.key(seed), 11)
    return {
        "inputs": scatter_about(key_of[0], (BATCH, SEQ, D), 1.0, 6.0, ((0, 2), (1, 8)), jnp.float32),
        "positions": draw_positions(jax.random.fold_in(key_of[10], 71), 0),
        "attn_gain": jnp.clip(1.0 + 0.1 * jax.random.normal(key_of[2], (LAYERS, D), jnp.float32), 0.5, 1.5).astype(jnp.bfloat16),
        "qkv_weight": scatter_about(key_of[3], (LAYERS, D, KV_HEADS * (GROUP + 2) * HEAD_DIM), D ** -0.5, 0.1875, ((1, 16), (2, 2))),
        "qkv_bias": draw_qkv_bias(jax.random.fold_in(key_of[10], 71), 0),
        "out_weight": scatter_about(key_of[5], (LAYERS, HEADS * HEAD_DIM, D), HEAD_DIM ** -0.5, 0.75, ((1, 2), (2, 16))),
        "ffn_gain": jnp.clip(1.0 + 0.1 * jax.random.normal(key_of[6], (LAYERS, D), jnp.float32), 0.5, 1.5).astype(jnp.bfloat16),
        "gate_up_weight": scatter_about(key_of[7], (LAYERS, D, 2, FF), D ** -0.5, 0.1875, ((1, 16), (3, 2))),
        "down_weight": scatter_about(key_of[8], (LAYERS, FF, D), FF ** -0.5, 0.078125, ((1, 2), (2, 16))),
        "cotangent": scatter_about(key_of[9], (BATCH, SEQ, D), 1.0, 6.0, ((0, 2), (1, 8)), jnp.float32),
    }


epsilon = 1e-06
base_theta = 1000000.0

def rope_tables(block_locations, head_dim):
    half_dim = head_dim // 2
    inv_freq = base_theta ** (-(jnp.arange(half_dim, dtype=jnp.float32) * 2.0) / head_dim)
    angles = block_locations.astype(jnp.float32)[:, None] * inv_freq[None, :]
    angles = jnp.concatenate([angles, angles], axis=1)
    return (jnp.cos(angles), jnp.sin(angles))

def rotate(values, cosine_lookup, sine_lookup):
    half_dim = values.shape[-1] // 2
    view_shape = (values.shape[0],) + (1,) * (values.ndim - 2) + (values.shape[-1],)
    turned = jnp.concatenate([-values[..., half_dim:], values[..., :half_dim]], axis=-1)
    return values * cosine_lookup.reshape(view_shape) + turned * sine_lookup.reshape(view_shape)

def rms_forward(hidden, gain_vec):
    scale_rows = lax.rsqrt(lax.optimization_barrier(jnp.mean(hidden * hidden, axis=-1, keepdims=True)) + epsilon)
    normed = hidden * scale_rows
    return (normed, scale_rows, (normed * gain_vec.astype(jnp.float32)).astype(jnp.bfloat16))

def rms_backward(grad_out, normed, scale_rows, gain_vec):
    gain_grad = lax.optimization_barrier(jnp.sum(grad_out * normed, axis=0))
    grad_normed = grad_out * gain_vec.astype(jnp.float32)
    grad_in = scale_rows * (grad_normed - normed * lax.optimization_barrier(jnp.mean(grad_normed * normed, axis=-1, keepdims=True)))
    return (grad_in, gain_grad)

def half_round(values):
    return lax.optimization_barrier(values.astype(jnp.bfloat16)).astype(jnp.float32)

def block_scores(query_block, key_float, place_block, block_locations):
    score_scale = query_block.shape[-1] ** (-0.5)
    scores = jnp.einsum('qcgd,kcd->cgqk', query_block.astype(jnp.float32), key_float) * score_scale
    allowed = (block_locations[None, :] <= place_block[:, None])[None, None]
    return (jnp.where(allowed, scores, -1e+30), allowed)

def attention_forward(query_heads, key_heads, value_heads, block_locations):
    seq_len = query_heads.shape[0]
    block_rows = min(512, seq_len)
    count_blocks = seq_len // block_rows
    key_float = key_heads.astype(jnp.float32)
    value_float = value_heads.astype(jnp.float32)

    def one_block(block_pair):
        query_block, place_block = block_pair
        scores, allowed = block_scores(query_block, key_float, place_block, block_locations)
        row_max = lax.optimization_barrier(jnp.max(scores, axis=-1, keepdims=True))
        row_total = lax.optimization_barrier(jnp.sum(jnp.where(allowed, jnp.exp(scores - row_max), 0.0), axis=-1, keepdims=True))
        log_total = row_max + jnp.log(row_total)
        prob_full = jnp.where(allowed, jnp.exp(scores - log_total), 0.0)
        attn_block = jnp.einsum('cgqk,kcd->qcgd', prob_full, value_float, precision=lax.Precision.HIGHEST).astype(jnp.bfloat16)
        return (attn_block, log_total[..., 0])
    query_blocks = query_heads.reshape((count_blocks, block_rows) + query_heads.shape[1:])
    attn_out, log_total = lax.map(one_block, (query_blocks, block_locations.reshape(count_blocks, block_rows)))
    return (attn_out.reshape(query_heads.shape), log_total)

def attention_backward(query_heads, key_heads, value_heads, block_locations, attn_out, log_total, grad_attn):
    seq_len = query_heads.shape[0]
    block_rows = min(512, seq_len)
    count_blocks = seq_len // block_rows
    score_scale = query_heads.shape[-1] ** (-0.5)
    key_float = key_heads.astype(jnp.float32)
    value_float = value_heads.astype(jnp.float32)

    def one_block(state_carry, items):
        key_grad, value_grad = state_carry
        query_block, place_block, attn_block, grad_block, log_block = items
        grad_float = grad_block.astype(jnp.float32)
        scores, allowed = block_scores(query_block, key_float, place_block, block_locations)
        probs = jnp.where(allowed, jnp.exp(scores - log_block[..., None]), 0.0)
        delta_rows = jnp.transpose(lax.optimization_barrier(jnp.sum(grad_float * attn_block.astype(jnp.float32), axis=-1)), (1, 2, 0))
        value_grad = value_grad + jnp.einsum('cgqk,qcgd->kcd', half_round(probs), grad_float)
        grad_probs = jnp.einsum('qcgd,kcd->cgqk', grad_float, value_float)
        grad_scores = half_round(probs * (grad_probs - delta_rows[..., None]))
        query_grad = jnp.einsum('cgqk,kcd->qcgd', grad_scores, key_float) * score_scale
        key_grad = key_grad + jnp.einsum('cgqk,qcgd->kcd', grad_scores, query_block.astype(jnp.float32)) * score_scale
        return ((key_grad, value_grad), query_grad)
    shape_blocks = (count_blocks, block_rows) + query_heads.shape[1:]
    initial = (jnp.zeros(key_heads.shape, jnp.float32), jnp.zeros(value_heads.shape, jnp.float32))
    items = (query_heads.reshape(shape_blocks), block_locations.reshape(count_blocks, block_rows), attn_out.reshape(shape_blocks), grad_attn.reshape(shape_blocks), log_total)
    (key_grad, value_grad), query_grad = lax.scan(one_block, initial, items)
    return (query_grad.reshape(query_heads.shape), key_grad, value_grad)

def layer_forward(hidden, block_locations, cosine_lookup, sine_lookup, weights):
    gain_attn, w_qkv, b_qkv, w_out, gain_ffn, w_gu, w_down = weights
    seq_len, model_width = hidden.shape
    ffn_width = w_down.shape[0]
    normed_a, scale_a, attn_in = rms_forward(hidden, gain_attn)
    qkv_proj = jnp.dot(attn_in, w_qkv, preferred_element_type=jnp.float32) + b_qkv.reshape(-1).astype(jnp.float32)
    qkv_proj = qkv_proj.reshape(seq_len, KV_HEADS, GROUP + 2, HEAD_DIM)
    query_heads = rotate(qkv_proj[:, :, :GROUP], cosine_lookup, sine_lookup).astype(jnp.bfloat16)
    key_heads = rotate(qkv_proj[:, :, GROUP], cosine_lookup, sine_lookup).astype(jnp.bfloat16)
    value_heads = qkv_proj[:, :, GROUP + 1].astype(jnp.bfloat16)
    attn_out, log_total = attention_forward(query_heads, key_heads, value_heads, block_locations)
    attn_flat = attn_out.reshape(seq_len, HEADS * HEAD_DIM)
    hidden_mid = hidden + jnp.dot(attn_flat, w_out, preferred_element_type=jnp.float32)
    normed_f, scale_f, ffn_in = rms_forward(hidden_mid, gain_ffn)
    gate_up_pre = jnp.dot(ffn_in, w_gu.reshape(model_width, 2 * ffn_width), preferred_element_type=jnp.float32)
    gate_pre = gate_up_pre[:, :ffn_width]
    up_pre = gate_up_pre[:, ffn_width:]
    mixed_units = (jax.nn.silu(gate_pre) * up_pre).astype(jnp.bfloat16)
    hidden_next = hidden_mid + jnp.dot(mixed_units, w_down, preferred_element_type=jnp.float32)
    saved_activations = (normed_a, scale_a, attn_in, query_heads, key_heads, value_heads, attn_out, log_total, attn_flat, normed_f, scale_f, ffn_in, gate_pre, up_pre, mixed_units)
    return (hidden_next, saved_activations)

def layer_reverse_pass(hidden_gradient, block_locations, cosine_lookup, sine_lookup, weights, saved_activations):
    gain_attn, w_qkv, b_qkv, w_out, gain_ffn, w_gu, w_down = weights
    normed_a, scale_a, attn_in, query_heads, key_heads, value_heads, attn_out, log_total, attn_flat, normed_f, scale_f, ffn_in, gate_pre, up_pre, mixed_units = saved_activations
    seq_len, model_width = hidden_gradient.shape
    ffn_width = w_down.shape[0]
    grad_half = hidden_gradient.astype(jnp.bfloat16)
    grad_mixed = jnp.dot(grad_half, w_down.T, preferred_element_type=jnp.float32)
    down_grad = jnp.dot(mixed_units.T, grad_half, preferred_element_type=jnp.float32)
    sigmoid_gate = jax.nn.sigmoid(gate_pre)
    silu_gate = gate_pre * sigmoid_gate
    grad_up = grad_mixed * silu_gate
    grad_gate = grad_mixed * up_pre * (sigmoid_gate + silu_gate * (1.0 - sigmoid_gate))
    grad_pre = jnp.concatenate([grad_gate, grad_up], axis=1).astype(jnp.bfloat16)
    gate_up_grad = jnp.dot(ffn_in.T, grad_pre, preferred_element_type=jnp.float32).reshape(model_width, 2, ffn_width)
    ffn_in_grad = jnp.dot(grad_pre, w_gu.reshape(model_width, 2 * ffn_width).T, preferred_element_type=jnp.float32)
    back_ffn, gain_ffn_grad = rms_backward(ffn_in_grad, normed_f, scale_f, gain_ffn)
    grad_mid = hidden_gradient + back_ffn
    grad_mid_half = grad_mid.astype(jnp.bfloat16)
    grad_attn = jnp.dot(grad_mid_half, w_out.T, preferred_element_type=jnp.float32).astype(jnp.bfloat16)
    out_grad = jnp.dot(attn_flat.T, grad_mid_half, preferred_element_type=jnp.float32)
    query_grad, key_grad, value_grad = attention_backward(query_heads, key_heads, value_heads, block_locations, attn_out, log_total, grad_attn.reshape(seq_len, KV_HEADS, GROUP, HEAD_DIM))
    query_grad = rotate(query_grad, cosine_lookup, -sine_lookup)
    key_grad = rotate(key_grad, cosine_lookup, -sine_lookup)
    grad_qkv = jnp.concatenate([query_grad, key_grad[:, :, None], value_grad[:, :, None]], axis=2)
    bias_grad = lax.optimization_barrier(jnp.sum(grad_qkv, axis=0)).reshape(KV_HEADS, (GROUP + 2) * HEAD_DIM)
    grad_qkv_half = grad_qkv.reshape(seq_len, KV_HEADS * (GROUP + 2) * HEAD_DIM).astype(jnp.bfloat16)
    qkv_grad = jnp.dot(attn_in.T, grad_qkv_half, preferred_element_type=jnp.float32)
    attn_in_grad = jnp.dot(grad_qkv_half, w_qkv.T, preferred_element_type=jnp.float32)
    back_attn, gain_attn_grad = rms_backward(attn_in_grad, normed_a, scale_a, gain_attn)
    grads = (gain_attn_grad, qkv_grad, bias_grad, out_grad, gain_ffn_grad, gate_up_grad, down_grad)
    return (grad_mid + back_attn, grads)

def reference(inputs, positions, attn_gain, qkv_weight, qkv_bias, out_weight, ffn_gain, gate_up_weight, down_weight, cotangent):
    layers = qkv_weight.shape[0]
    layer_weight_groups = [(attn_gain[layer_index], qkv_weight[layer_index], qkv_bias[layer_index], out_weight[layer_index], ffn_gain[layer_index], gate_up_weight[layer_index], down_weight[layer_index]) for layer_index in range(layers)]
    outputs = []
    input_grads = []
    grad_sums = None
    for seq_idx in range(inputs.shape[0]):
        block_locations = positions[seq_idx]
        cosine_lookup, sine_lookup = rope_tables(block_locations, HEAD_DIM)
        hidden = inputs[seq_idx]
        saved_activation_list = []
        for layer_index in range(layers):
            hidden, saved_activations = layer_forward(hidden, block_locations, cosine_lookup, sine_lookup, layer_weight_groups[layer_index])
            saved_activation_list.append(saved_activations)
        outputs.append(hidden)
        hidden_gradient = cotangent[seq_idx]
        layer_gradient_list = [None] * layers
        for layer_index in reversed(range(layers)):
            hidden_gradient, layer_gradient_list[layer_index] = layer_reverse_pass(hidden_gradient, block_locations, cosine_lookup, sine_lookup, layer_weight_groups[layer_index], saved_activation_list[layer_index])
        input_grads.append(hidden_gradient)
        stacked = tuple((jnp.stack([layer_gradient_list[layer_index][member] for layer_index in range(layers)]) for member in range(7)))
        grad_sums = stacked if grad_sums is None else jax.tree.map(jnp.add, grad_sums, stacked)
    return (jnp.stack(outputs), jnp.stack(input_grads), grad_sums[0], grad_sums[1], grad_sums[2], grad_sums[3], grad_sums[4], grad_sums[5], grad_sums[6])
```

```python
import jax
import jax.numpy as jnp
from jax import lax
from jax.sharding import PartitionSpec as P

HEAD_DIM = 64
GROUP = 7
LANES = 128

epsilon = 1e-06
base_theta = 1000000.0


f32 = jnp.float32
bf16 = jnp.bfloat16


def rope_tables(block_locations, head_dim):
    half_dim = head_dim // 2
    inv_freq = base_theta ** (-(jnp.arange(half_dim, dtype=f32) * 2.0) / head_dim)
    angles = block_locations.astype(f32)[:, None] * inv_freq[None, :]
    angles = jnp.concatenate([angles, angles], axis=1)
    return (jnp.cos(angles), jnp.sin(angles))


def rotate(values, cosine_lookup, sine_lookup):
    half_dim = values.shape[-1] // 2
    view_shape = (values.shape[0],) + (1,) * (values.ndim - 2) + (values.shape[-1],)
    turned = jnp.concatenate([-values[..., half_dim:], values[..., :half_dim]], axis=-1)
    return values * cosine_lookup.reshape(view_shape) + turned * sine_lookup.reshape(view_shape)


def rms_forward(hidden, gain_vec):
    scale_rows = lax.rsqrt(jnp.mean(hidden * hidden, axis=-1, keepdims=True) + epsilon)
    normed = hidden * scale_rows
    return (normed, scale_rows, (normed * gain_vec.astype(f32)).astype(bf16))


def rms_backward(grad_out, normed, scale_rows, gain_vec):
    gain_grad = jnp.sum(grad_out * normed, axis=0)
    grad_normed = grad_out * gain_vec.astype(f32)
    grad_in = scale_rows * (
        grad_normed - normed * jnp.mean(grad_normed * normed, axis=-1, keepdims=True)
    )
    return (grad_in, gain_grad)


def dot_nt(a, b):
    return lax.dot_general(a, b, (((1,), (1,)), ((), ())), preferred_element_type=f32)


def dot_tn(a, b):
    return lax.dot_general(a, b, (((0,), (0,)), ((), ())), preferred_element_type=f32)


def dot_nn(a, b):
    return jnp.dot(a, b, preferred_element_type=f32)


def make_local(n_dp, n_ctx, n_mp):
    n_lo = 2
    n_hi = n_ctx // n_lo
    assert n_dp == 2 and n_mp == 2 and n_hi * n_lo == n_ctx
    pair = [(0, 1), (1, 0)]
    lo_pair = [(i, i ^ 1) for i in range(n_ctx)]

    def swap_dp(v):
        return lax.ppermute(v, "dp", pair)

    def swap_mp(v):
        return lax.ppermute(v, "mp", pair)

    def swap_lo(v):
        return lax.ppermute(v, "ctx", lo_pair)

    def shift_hi(v, k):
        return lax.ppermute(
            v,
            "ctx",
            [(h * n_lo + e, (h + k) % n_hi * n_lo + e) for h in range(n_hi) for e in range(n_lo)],
        )

    def in_order(flag, own, other):
        first = flag == 0
        return jnp.stack([jnp.where(first, own, other), jnp.where(first, other, own)])

    def pick(flag, two):
        first = flag == 0
        return jnp.where(first, two[0], two[1]), jnp.where(first, two[1], two[0])

    def gather_hi(block, hi):
        got = jnp.stack([block] + [shift_hi(block, k) for k in range(1, n_hi)])
        return jnp.stack(
            [
                lax.dynamic_index_in_dim(got, (hi - j) % n_hi, 0, keepdims=False)
                for j in range(n_hi)
            ]
        )

    def scatter_hi(parts, hi):
        total = lax.dynamic_index_in_dim(parts, hi, 0, keepdims=False).astype(f32)
        for k in range(1, n_hi):
            part = lax.dynamic_index_in_dim(parts, (hi + k) % n_hi, 0, keepdims=False)
            total = total + shift_hi(part, k).astype(f32)
        return total

    def gather_rows(block, c, hi, lo):
        both = in_order(lo, block, swap_lo(block))
        mine = gather_hi(both, hi)
        return in_order(c, mine, swap_dp(mine))

    def scatter_rows(parts, c, hi, lo):
        keep, send = pick(c, parts)
        keep = keep + swap_dp(send.astype(bf16)).astype(f32)
        mine = scatter_hi(keep.astype(bf16), hi)
        keep, send = pick(lo, mine)
        return keep + swap_lo(send.astype(bf16)).astype(f32)

    def gather_plane(block, c, lo):
        both = in_order(lo, block, swap_lo(block))
        return in_order(c, both, swap_dp(both))

    def scatter_plane(parts, c, lo):
        keep, send = pick(c, parts)
        keep = keep + swap_dp(send.astype(bf16)).astype(f32)
        keep, send = pick(lo, keep)
        keep = keep + swap_lo(send.astype(bf16)).astype(f32)
        return sum_mp(keep)

    def sum_mp(part):
        part = part.astype(bf16)
        return part.astype(f32) + swap_mp(part).astype(f32)

    def local(
        inputs,
        positions,
        attn_gain,
        qkv_weight,
        qkv_bias,
        out_weight,
        ffn_gain,
        gate_up_weight,
        down_weight,
        cotangent,
    ):
        c = lax.axis_index("dp")
        ctx = lax.axis_index("ctx")
        hi, lo = ctx // n_lo, ctx % n_lo
        tokens = inputs.shape[1]
        model_width = inputs.shape[2]
        head_dim = HEAD_DIM
        group_size = GROUP
        score_scale = head_dim ** (-0.5)
        rows = qkv_weight.shape[1]
        units = down_weight.shape[1]
        splits = n_dp * n_lo
        piece = -(-units // (splits * LANES)) * LANES
        n_shards = n_dp * n_ctx

        seq_pos = positions[0]
        my_pos = lax.dynamic_slice_in_dim(seq_pos, ctx * tokens, tokens)
        row_pos = jnp.tile(my_pos, group_size)
        cosine_lookup, sine_lookup = rope_tables(my_pos, head_dim)
        hidden = inputs[0]

        w_q = qkv_weight[0]
        width_q = w_q.shape[1]
        gain_cols = -(-rows // LANES) * LANES
        bias_cols = qkv_bias.shape[2]
        extra = jnp.concatenate(
            [
                jnp.pad(attn_gain[0], (0, gain_cols - rows)),
                jnp.pad(ffn_gain[0], (0, gain_cols - rows)),
                jnp.pad(qkv_bias[0, 0], (0, width_q - 2 * gain_cols - bias_cols)),
            ]
        )[None]
        extra = jnp.pad(extra, ((0, 7), (0, 0)))
        got_q = gather_rows(jnp.concatenate([w_q, extra], axis=0), c, hi, lo)
        got_q = got_q.reshape(n_shards, rows + 8, width_q)
        w_qkv = got_q[:, :rows].reshape(model_width, width_q)
        side = got_q[:, rows]
        gain_attn = side[:, :rows].reshape(model_width)
        gain_ffn = side[:, gain_cols : gain_cols + rows].reshape(model_width)
        b_qkv = side[:, 2 * gain_cols : 2 * gain_cols + bias_cols].reshape(width_q)

        shards = [gate_up_weight[0, :, 0], gate_up_weight[0, :, 1], down_weight[0].T]
        shards = [jnp.pad(s, ((0, 0), (0, splits * piece - units))) for s in shards]
        groups = [
            jnp.concatenate([s[:, q * piece : (q + 1) * piece] for s in shards], axis=1)
            for q in range(splits)
        ]
        halves = [jnp.stack(groups[e * n_dp : (e + 1) * n_dp]) for e in range(n_lo)]
        keep, send = pick(lo, halves)
        both = in_order(lo, keep, swap_lo(send))
        keep, send = pick(c, (both[:, 0], both[:, 1]))
        plane = in_order(c, keep, swap_dp(send))
        w_ffn = gather_hi(plane, hi)
        w_ffn = jnp.transpose(w_ffn, (1, 0, 2, 3, 4)).reshape(model_width, 3 * piece)
        w_gu, w_dt = w_ffn[:, : 2 * piece], w_ffn[:, 2 * piece :]

        w_ot = gather_rows(out_weight[0].T, c, hi, lo).reshape(model_width, -1)

        grad_out = cotangent[0]
        grad_half = gather_plane(grad_out.astype(bf16), c, lo).reshape(-1, model_width)

        normed_a, scale_a, attn_in = rms_forward(hidden, gain_attn)
        qkv_proj = dot_nn(attn_in, w_qkv) + b_qkv.astype(f32)
        qkv_proj = qkv_proj.reshape(tokens, group_size + 2, head_dim)
        query_heads = rotate(qkv_proj[:, :group_size], cosine_lookup, sine_lookup).astype(bf16)
        key_head = rotate(
            qkv_proj[:, group_size : group_size + 1], cosine_lookup, sine_lookup
        )[:, 0].astype(bf16)
        value_head = qkv_proj[:, group_size + 1].astype(bf16)
        query_rows = jnp.transpose(query_heads, (1, 0, 2)).reshape(group_size * tokens, head_dim)
        pair_kv = jnp.concatenate([key_head, value_head], axis=1)
        pair_kv = jnp.broadcast_to(pair_kv[None], (n_ctx,) + pair_kv.shape)
        pair_kv = lax.all_to_all(pair_kv, "ctx", 0, 0, tiled=True).reshape(-1, 2 * head_dim)
        key_all, value_all = pair_kv[:, :head_dim], pair_kv[:, head_dim:]
        allowed = seq_pos[None, :] <= row_pos[:, None]
        scores = jnp.where(allowed, dot_nt(query_rows, key_all) * score_scale, -1e30)
        row_max = jnp.max(scores, axis=1)
        weights_now = jnp.where(allowed, jnp.exp(scores - row_max[:, None]), 0.0)
        row_total = jnp.sum(weights_now, axis=1)
        row_accum = jnp.dot(
            weights_now,
            value_all.astype(f32),
            precision=lax.Precision.HIGHEST,
            preferred_element_type=f32,
        )
        log_total = row_max + jnp.log(row_total)
        attn_rows = (row_accum / row_total[:, None]).astype(bf16)
        attn_flat = jnp.transpose(
            attn_rows.reshape(group_size, tokens, head_dim), (1, 0, 2)
        ).reshape(tokens, group_size * head_dim)
        hidden_mid = hidden + sum_mp(dot_nt(attn_flat, w_ot))

        normed_f, scale_f, ffn_in = rms_forward(hidden_mid, gain_ffn)
        ffn_all = gather_plane(ffn_in, c, lo).reshape(-1, model_width)
        gate_up_pre = dot_nn(ffn_all, w_gu)
        gate_pre, up_pre = gate_up_pre[:, :piece], gate_up_pre[:, piece:]
        grad_mixed = dot_nn(grad_half, w_dt)
        sigmoid_gate = jax.nn.sigmoid(gate_pre)
        silu_gate = gate_pre * sigmoid_gate
        mixed_units = (silu_gate * up_pre).astype(bf16)
        grad_up = grad_mixed * silu_gate
        grad_gate = grad_mixed * up_pre * (sigmoid_gate + silu_gate * (1.0 - sigmoid_gate))
        grad_pre = jnp.concatenate([grad_gate, grad_up], axis=1).astype(bf16)
        plane_shape = (n_dp, n_lo, tokens, model_width)
        ffn_in_part = dot_nt(grad_pre, w_gu).reshape(plane_shape)
        ffn_in_grad = scatter_plane(ffn_in_part, c, lo)
        ffn_part = dot_nt(mixed_units, w_dt).reshape(plane_shape)
        hidden_next = hidden_mid + scatter_plane(ffn_part, c, lo)
        w_grad = jnp.concatenate(
            [dot_tn(ffn_all, grad_pre), dot_tn(grad_half, mixed_units)], axis=1
        ).astype(bf16)
        w_grad = w_grad.reshape(n_dp, n_hi, n_lo, rows, 3 * piece)
        w_grad = scatter_hi(jnp.transpose(w_grad, (1, 0, 2, 3, 4)), hi).astype(bf16)
        keep, send = pick(c, w_grad)
        by_c = in_order(c, keep, swap_dp(send))
        keep, send = pick(lo, (by_c[:, 0], by_c[:, 1]))
        by_q = in_order(lo, keep, swap_lo(send)).reshape(splits, rows, 3 * piece).astype(f32)
        gate_grad, up_grad, down_grad = [
            jnp.concatenate(
                [by_q[q, :, e * piece : (e + 1) * piece] for q in range(splits)], axis=1
            )[:, :units]
            for e in range(3)
        ]

        back_ffn, gain_ffn_part = rms_backward(ffn_in_grad, normed_f, scale_f, gain_ffn)
        grad_mid = grad_out + back_ffn
        grad_mid_half = grad_mid.astype(bf16)
        grad_attn = dot_nn(grad_mid_half, w_ot).astype(bf16)
        out_part = dot_tn(grad_mid_half, attn_flat)
        grad_rows = jnp.transpose(
            grad_attn.reshape(tokens, group_size, head_dim), (1, 0, 2)
        ).reshape(group_size * tokens, head_dim)
        delta_rows = jnp.sum(grad_rows.astype(f32) * attn_rows.astype(f32), axis=1)
        probs = jnp.where(allowed, jnp.exp(scores - log_total[:, None]), 0.0)
        value_grad_all = dot_tn(probs.astype(bf16), grad_rows)
        grad_probs = dot_nt(grad_rows, value_all)
        grad_scores = (probs * (grad_probs - delta_rows[:, None])).astype(bf16)
        query_grad = dot_nn(grad_scores, key_all) * score_scale
        key_grad_all = dot_tn(grad_scores, query_rows) * score_scale
        kv_grad = jnp.concatenate([key_grad_all, value_grad_all], axis=1).astype(bf16)
        kv_grad = lax.all_to_all(
            kv_grad.reshape(n_ctx, tokens, 2 * head_dim), "ctx", 0, 0, tiled=True
        )
        kv_grad = jnp.sum(kv_grad.astype(f32), axis=0)
        key_grad, value_grad = kv_grad[:, :head_dim], kv_grad[:, head_dim:]
        query_grad = jnp.transpose(query_grad.reshape(group_size, tokens, head_dim), (1, 0, 2))
        query_grad = rotate(query_grad, cosine_lookup, -sine_lookup)
        key_grad = rotate(key_grad[:, None], cosine_lookup, -sine_lookup)
        grad_qkv = jnp.concatenate([query_grad, key_grad, value_grad[:, None]], axis=1).reshape(
            tokens, (group_size + 2) * head_dim
        )
        bias_part = jnp.sum(grad_qkv, axis=0)
        grad_qkv_half = grad_qkv.astype(bf16)
        attn_in_grad = sum_mp(dot_nt(grad_qkv_half, w_qkv))
        back_attn, gain_attn_part = rms_backward(attn_in_grad, normed_a, scale_a, gain_attn)
        input_grad = grad_mid + back_attn
        qkv_part = dot_tn(attn_in, grad_qkv_half).reshape(n_shards, rows, width_q)

        out_grad = scatter_rows(
            out_part.reshape(n_dp, n_hi, n_lo, rows, -1), c, hi, lo
        )
        extra = jnp.concatenate(
            [
                jnp.pad(gain_attn_part.reshape(n_shards, rows), ((0, 0), (0, gain_cols - rows))),
                jnp.pad(gain_ffn_part.reshape(n_shards, rows), ((0, 0), (0, gain_cols - rows))),
                jnp.pad(
                    bias_part.reshape(n_shards, bias_cols),
                    ((0, 0), (0, width_q - 2 * gain_cols - bias_cols)),
                ),
            ],
            axis=1,
        )
        extra = jnp.pad(extra[:, None], ((0, 0), (0, 7), (0, 0)))
        qkv_part = jnp.concatenate([qkv_part, extra], axis=1)
        qkv_sum = scatter_rows(
            qkv_part.reshape(n_dp, n_hi, n_lo, rows + 8, width_q), c, hi, lo
        )
        side = qkv_sum[rows]
        return (
            hidden_next[None],
            input_grad[None],
            side[:rows][None],
            qkv_sum[:rows][None],
            side[2 * gain_cols : 2 * gain_cols + bias_cols][None, None],
            out_grad.T[None],
            side[gain_cols : gain_cols + rows][None],
            jnp.stack([gate_grad, up_grad], axis=1)[None],
            down_grad.T[None],
        )

    return local


def solution(mesh):
    both = ("dp", "ctx")
    return jax.shard_map(
        make_local(mesh.shape["dp"], mesh.shape["ctx"], mesh.shape["mp"]),
        mesh=mesh,
        in_specs=(
            P("dp", "ctx", None),
            P("dp", None),
            P(None, both),
            P(None, both, "mp"),
            P(None, "mp", both),
            P(None, "mp", both),
            P(None, both),
            P(None, both, None, "mp"),
            P(None, "mp", both),
            P("dp", "ctx", None),
        ),
        out_specs=(
            P("dp", "ctx", None),
            P("dp", "ctx", None),
            P(None, both),
            P(None, both, "mp"),
            P(None, "mp", both),
            P(None, "mp", both),
            P(None, both),
            P(None, both, None, "mp"),
            P(None, "mp", both),
        ),
        check_vma=False,
    )
```

```python
import jax
import jax.numpy as jnp
from jax import lax
from jax.sharding import PartitionSpec as P

HEAD_DIM = 64
GROUP = 7
LANES = 128

epsilon = 1e-06
base_theta = 1000000.0


f32 = jnp.float32
bf16 = jnp.bfloat16


def rope_tables(block_locations, head_dim):
    half_dim = head_dim // 2
    inv_freq = base_theta ** (-(jnp.arange(half_dim, dtype=f32) * 2.0) / head_dim)
    angles = block_locations.astype(f32)[:, None] * inv_freq[None, :]
    angles = jnp.concatenate([angles, angles], axis=1)
    return (jnp.cos(angles), jnp.sin(angles))


def rotate(values, cosine_lookup, sine_lookup):
    half_dim = values.shape[-1] // 2
    view_shape = (values.shape[0],) + (1,) * (values.ndim - 2) + (values.shape[-1],)
    turned = jnp.concatenate([-values[..., half_dim:], values[..., :half_dim]], axis=-1)
    return values * cosine_lookup.reshape(view_shape) + turned * sine_lookup.reshape(view_shape)


def rms_forward(hidden, gain_vec):
    scale_rows = lax.rsqrt(jnp.mean(hidden * hidden, axis=-1, keepdims=True) + epsilon)
    normed = hidden * scale_rows
    return (normed, scale_rows, (normed * gain_vec.astype(f32)).astype(bf16))


def rms_backward(grad_out, normed, scale_rows, gain_vec):
    gain_grad = jnp.sum(grad_out * normed, axis=0)
    grad_normed = grad_out * gain_vec.astype(f32)
    grad_in = scale_rows * (
        grad_normed - normed * jnp.mean(grad_normed * normed, axis=-1, keepdims=True)
    )
    return (grad_in, gain_grad)


def after(value, *others):
    return lax.optimization_barrier((value,) + others)[0]


def dot_nt(a, b):
    return lax.dot_general(a, b, (((1,), (1,)), ((), ())), preferred_element_type=f32)


def dot_tn(a, b):
    return lax.dot_general(a, b, (((0,), (0,)), ((), ())), preferred_element_type=f32)


def dot_nn(a, b):
    return jnp.dot(a, b, preferred_element_type=f32)


def make_local(n_dp, n_ctx, n_mp):
    n_lo = 2
    n_hi = n_ctx // n_lo
    assert n_dp == 2 and n_mp == 2 and n_hi * n_lo == n_ctx
    pair = [(0, 1), (1, 0)]
    lo_pair = [(i, i ^ 1) for i in range(n_ctx)]

    def swap_dp(v):
        return lax.ppermute(v, "dp", pair)

    def swap_mp(v):
        return lax.ppermute(v, "mp", pair)

    def swap_lo(v):
        return lax.ppermute(v, "ctx", lo_pair)

    def swap_hi(v, mask):
        return lax.ppermute(
            v, "ctx", [(h * n_lo + e, (h ^ mask) * n_lo + e) for h in range(n_hi) for e in range(n_lo)]
        )

    def in_order(flag, own, other):
        first = flag == 0
        return jnp.stack([jnp.where(first, own, other), jnp.where(first, other, own)])

    def pick(flag, two):
        first = flag == 0
        return jnp.where(first, two[0], two[1]), jnp.where(first, two[1], two[0])

    def by_mask(got, hi):
        got = jnp.stack(got)
        return jnp.stack(
            [
                lax.dynamic_index_in_dim(got, jnp.bitwise_xor(hi, j), 0, keepdims=False)
                for j in range(n_hi)
            ]
        )

    def gather_hi(block, hi):
        return by_mask([block] + [swap_hi(block, k) for k in range(1, n_hi)], hi)

    def relay_masks():
        masks, step = [], n_hi // 2
        while step:
            masks.append(step)
            step //= 2
        return masks

    def scatter_hi(parts, hi):
        total = lax.dynamic_index_in_dim(parts, hi, 0, keepdims=False).astype(f32)
        for k in range(1, n_hi):
            part = lax.dynamic_index_in_dim(parts, jnp.bitwise_xor(hi, k), 0, keepdims=False)
            total = total + swap_hi(part, k).astype(f32)
        return total

    def gather_rows(both, c, hi):
        mine = gather_hi(both, hi)
        return in_order(c, mine, swap_dp(mine))

    def scatter_rows(parts, c, hi, lo):
        keep, send = pick(c, parts)
        keep = keep + swap_dp(send.astype(bf16)).astype(f32)
        mine = scatter_hi(keep.astype(bf16), hi)
        keep, send = pick(lo, mine)
        return keep + swap_lo(send.astype(bf16)).astype(f32)

    def gather_lo(block, lo):
        return in_order(lo, block, swap_lo(block))

    def gather_dp(block, c):
        return in_order(c, block, swap_dp(block))

    def scatter_plane(parts, c, lo):
        keep, send = pick(c, parts)
        keep = keep + swap_dp(send.astype(bf16)).astype(f32)
        keep, send = pick(lo, keep)
        keep = keep + swap_lo(send.astype(bf16)).astype(f32)
        return sum_mp(keep)

    def sum_mp(part):
        part = part.astype(bf16)
        return part.astype(f32) + swap_mp(part).astype(f32)

    def local(
        inputs,
        positions,
        attn_gain,
        qkv_weight,
        qkv_bias,
        out_weight,
        ffn_gain,
        gate_up_weight,
        down_weight,
        cotangent,
    ):
        c = lax.axis_index("dp")
        ctx = lax.axis_index("ctx")
        hi, lo = ctx // n_lo, ctx % n_lo
        tokens = inputs.shape[1]
        model_width = inputs.shape[2]
        head_dim = HEAD_DIM
        group_size = GROUP
        score_scale = head_dim ** (-0.5)
        rows = qkv_weight.shape[1]
        units = down_weight.shape[1]
        splits = n_dp * n_lo
        piece = -(-units // (splits * LANES)) * LANES
        n_shards = n_dp * n_ctx

        seq_pos = positions[0]
        my_pos = lax.dynamic_slice_in_dim(seq_pos, ctx * tokens, tokens)
        row_pos = jnp.tile(my_pos, group_size)
        cosine_lookup, sine_lookup = rope_tables(my_pos, head_dim)
        hidden = inputs[0]

        w_q = qkv_weight[0]
        width_q = w_q.shape[1]
        gain_cols = -(-rows // LANES) * LANES
        bias_cols = qkv_bias.shape[2]
        extra = jnp.concatenate(
            [
                jnp.pad(attn_gain[0], (0, gain_cols - rows)),
                jnp.pad(ffn_gain[0], (0, gain_cols - rows)),
                jnp.pad(qkv_bias[0, 0], (0, width_q - 2 * gain_cols - bias_cols)),
            ]
        )[None]
        extra = jnp.pad(extra, ((0, 7), (0, 0)))
        both_q = gather_lo(jnp.concatenate([w_q, extra], axis=0), lo)
        got_q = gather_rows(both_q, c, hi).reshape(n_shards, rows + 8, width_q)
        w_qkv = got_q[:, :rows].reshape(model_width, width_q)
        side = got_q[:, rows]
        gain_attn = side[:, :rows].reshape(model_width)
        gain_ffn = side[:, gain_cols : gain_cols + rows].reshape(model_width)
        b_qkv = side[:, 2 * gain_cols : 2 * gain_cols + bias_cols].reshape(width_q)

        shards = [gate_up_weight[0, :, 0], gate_up_weight[0, :, 1], down_weight[0].T]
        shards = [jnp.pad(s, ((0, 0), (0, splits * piece - units))) for s in shards]
        groups = [
            jnp.concatenate([s[:, q * piece : (q + 1) * piece] for s in shards], axis=1)
            for q in range(splits)
        ]
        halves = [jnp.stack(groups[e * n_dp : (e + 1) * n_dp]) for e in range(n_lo)]
        keep, send = pick(lo, halves)
        both = in_order(lo, keep, swap_lo(after(send, both_q)))
        both_o = gather_lo(after(out_weight[0].T, both_q), lo)
        grad_out = cotangent[0]
        grad_pair = gather_lo(after(grad_out.astype(bf16), both, both_o), lo)
        grad_half = gather_dp(grad_pair, c).reshape(-1, model_width)
        keep, send = pick(c, (both[:, 0], both[:, 1]))
        plane = in_order(c, keep, swap_dp(send))
        w_ot = gather_rows(after(both_o, got_q), c, hi).reshape(model_width, -1)
        plane = after(plane, got_q)
        relayed = {0: plane}
        for mask in relay_masks():
            for k in list(relayed):
                relayed[k ^ mask] = swap_hi(relayed[k], mask)
        w_ffn = by_mask([relayed[k] for k in range(n_hi)], hi)
        w_ffn = jnp.transpose(w_ffn, (1, 0, 2, 3, 4)).reshape(model_width, 3 * piece)
        w_gu, w_dt = w_ffn[:, : 2 * piece], w_ffn[:, 2 * piece :]

        normed_a, scale_a, attn_in = rms_forward(hidden, gain_attn)
        qkv_proj = dot_nn(attn_in, w_qkv) + b_qkv.astype(f32)
        qkv_proj = qkv_proj.reshape(tokens, group_size + 2, head_dim)
        query_heads = rotate(qkv_proj[:, :group_size], cosine_lookup, sine_lookup).astype(bf16)
        key_head = rotate(
            qkv_proj[:, group_size : group_size + 1], cosine_lookup, sine_lookup
        )[:, 0].astype(bf16)
        value_head = qkv_proj[:, group_size + 1].astype(bf16)
        query_rows = jnp.transpose(query_heads, (1, 0, 2)).reshape(group_size * tokens, head_dim)
        pair_kv = jnp.concatenate([key_head, value_head], axis=1)
        pair_kv = jnp.broadcast_to(pair_kv[None], (n_ctx,) + pair_kv.shape)
        pair_kv = lax.all_to_all(pair_kv, "ctx", 0, 0, tiled=True).reshape(-1, 2 * head_dim)
        key_all, value_all = pair_kv[:, :head_dim], pair_kv[:, head_dim:]
        allowed = seq_pos[None, :] <= row_pos[:, None]
        scores = jnp.where(allowed, dot_nt(query_rows, key_all) * score_scale, -1e30)
        row_max = jnp.max(scores, axis=1)
        weights_now = jnp.where(allowed, jnp.exp(scores - row_max[:, None]), 0.0)
        row_total = jnp.sum(weights_now, axis=1)
        row_accum = jnp.dot(
            weights_now,
            value_all.astype(f32),
            precision=lax.Precision.HIGHEST,
            preferred_element_type=f32,
        )
        log_total = row_max + jnp.log(row_total)
        attn_rows = (row_accum / row_total[:, None]).astype(bf16)
        attn_flat = jnp.transpose(
            attn_rows.reshape(group_size, tokens, head_dim), (1, 0, 2)
        ).reshape(tokens, group_size * head_dim)
        hidden_mid = hidden + sum_mp(dot_nt(attn_flat, w_ot))

        normed_f, scale_f, ffn_in = rms_forward(hidden_mid, gain_ffn)
        ffn_all = gather_dp(gather_lo(ffn_in, lo), c).reshape(-1, model_width)
        gate_up_pre = dot_nn(ffn_all, w_gu)
        gate_pre, up_pre = gate_up_pre[:, :piece], gate_up_pre[:, piece:]
        grad_mixed = dot_nn(grad_half, w_dt)
        sigmoid_gate = jax.nn.sigmoid(gate_pre)
        silu_gate = gate_pre * sigmoid_gate
        mixed_units = (silu_gate * up_pre).astype(bf16)
        grad_up = grad_mixed * silu_gate
        grad_gate = grad_mixed * up_pre * (sigmoid_gate + silu_gate * (1.0 - sigmoid_gate))
        grad_pre = jnp.concatenate([grad_gate, grad_up], axis=1).astype(bf16)
        plane_shape = (n_dp, n_lo, tokens, model_width)
        ffn_in_part = dot_nt(grad_pre, w_gu).reshape(plane_shape)
        ffn_in_grad = scatter_plane(ffn_in_part, c, lo)
        ffn_part = dot_nt(mixed_units, w_dt).reshape(plane_shape)
        hidden_next = hidden_mid + scatter_plane(ffn_part, c, lo)
        w_grad = jnp.concatenate(
            [dot_tn(ffn_all, grad_pre), dot_tn(grad_half, mixed_units)], axis=1
        ).astype(bf16)
        w_grad = w_grad.reshape(n_dp, n_hi, n_lo, rows, 3 * piece)
        w_grad = jnp.transpose(w_grad, (1, 0, 2, 3, 4))
        parts = [
            lax.dynamic_index_in_dim(w_grad, jnp.bitwise_xor(hi, k), 0, keepdims=False)
            for k in range(n_hi)
        ]
        sums = {k: [part] for k, part in enumerate(parts)}
        for mask in reversed(relay_masks()):
            for k in sorted(sums, reverse=True):
                if k & mask:
                    moved = sums.pop(k)
                    moved = moved[0] if len(moved) == 1 else sum(
                        m.astype(f32) for m in moved
                    ).astype(bf16)
                    sums[k ^ mask].append(swap_hi(moved, mask))

        back_ffn, gain_ffn_part = rms_backward(ffn_in_grad, normed_f, scale_f, gain_ffn)
        grad_mid = grad_out + back_ffn
        grad_mid_half = grad_mid.astype(bf16)
        grad_attn = dot_nn(grad_mid_half, w_ot).astype(bf16)
        out_part = dot_tn(grad_mid_half, attn_flat)
        grad_rows = jnp.transpose(
            grad_attn.reshape(tokens, group_size, head_dim), (1, 0, 2)
        ).reshape(group_size * tokens, head_dim)
        delta_rows = jnp.sum(grad_rows.astype(f32) * attn_rows.astype(f32), axis=1)
        probs = jnp.where(allowed, jnp.exp(scores - log_total[:, None]), 0.0)
        value_grad_all = dot_tn(probs.astype(bf16), grad_rows)
        grad_probs = dot_nt(grad_rows, value_all)
        grad_scores = (probs * (grad_probs - delta_rows[:, None])).astype(bf16)
        query_grad = dot_nn(grad_scores, key_all) * score_scale
        key_grad_all = dot_tn(grad_scores, query_rows) * score_scale
        kv_grad = jnp.concatenate([key_grad_all, value_grad_all], axis=1).astype(bf16)
        kv_grad = lax.all_to_all(
            kv_grad.reshape(n_ctx, tokens, 2 * head_dim), "ctx", 0, 0, tiled=True
        )
        kv_grad = jnp.sum(kv_grad.astype(f32), axis=0)
        key_grad, value_grad = kv_grad[:, :head_dim], kv_grad[:, head_dim:]
        query_grad = jnp.transpose(query_grad.reshape(group_size, tokens, head_dim), (1, 0, 2))
        query_grad = rotate(query_grad, cosine_lookup, -sine_lookup)
        key_grad = rotate(key_grad[:, None], cosine_lookup, -sine_lookup)
        grad_qkv = jnp.concatenate([query_grad, key_grad, value_grad[:, None]], axis=1).reshape(
            tokens, (group_size + 2) * head_dim
        )
        bias_part = jnp.sum(grad_qkv, axis=0)
        grad_qkv_half = grad_qkv.astype(bf16)
        attn_in_grad = sum_mp(dot_nt(grad_qkv_half, w_qkv))
        back_attn, gain_attn_part = rms_backward(attn_in_grad, normed_a, scale_a, gain_attn)
        input_grad = grad_mid + back_attn
        qkv_part = dot_tn(attn_in, grad_qkv_half)

        out_grad = scatter_rows(
            out_part.reshape(n_dp, n_hi, n_lo, rows, -1), c, hi, lo
        )
        qkv_sum = scatter_rows(qkv_part.reshape(n_dp, n_hi, n_lo, rows, width_q), c, hi, lo)
        side = jnp.stack(
            [
                jnp.pad(v.reshape(n_shards, -1), ((0, 0), (0, gain_cols - v.shape[0] // n_shards)))
                for v in (gain_attn_part, gain_ffn_part, bias_part)
            ],
            axis=1,
        )
        side = jnp.pad(side, ((0, 0), (0, 5), (0, 0)))
        side = jnp.sum(lax.all_to_all(side, ("dp", "ctx"), 0, 0, tiled=True), axis=0)

        w_grad = sum(after(m, grad_qkv_half).astype(f32) for m in sums[0]).astype(bf16)
        keep, send = pick(c, w_grad)
        by_c = in_order(c, keep, swap_dp(send))
        keep, send = pick(lo, (by_c[:, 0], by_c[:, 1]))
        by_q = in_order(lo, keep, swap_lo(send)).reshape(splits, rows, 3 * piece).astype(f32)
        gate_grad, up_grad, down_grad = [
            jnp.concatenate(
                [by_q[q, :, e * piece : (e + 1) * piece] for q in range(splits)], axis=1
            )[:, :units]
            for e in range(3)
        ]
        return (
            hidden_next[None],
            input_grad[None],
            side[:1, :rows],
            qkv_sum[None],
            side[2:3, :bias_cols][None],
            out_grad.T[None],
            side[1:2, :rows],
            jnp.stack([gate_grad, up_grad], axis=1)[None],
            down_grad.T[None],
        )

    return local


def solution(mesh):
    both = ("dp", "ctx")
    return jax.shard_map(
        make_local(mesh.shape["dp"], mesh.shape["ctx"], mesh.shape["mp"]),
        mesh=mesh,
        in_specs=(
            P("dp", "ctx", None),
            P("dp", None),
            P(None, both),
            P(None, both, "mp"),
            P(None, "mp", both),
            P(None, "mp", both),
            P(None, both),
            P(None, both, None, "mp"),
            P(None, "mp", both),
            P("dp", "ctx", None),
        ),
        out_specs=(
            P("dp", "ctx", None),
            P("dp", "ctx", None),
            P(None, both),
            P(None, both, "mp"),
            P(None, "mp", both),
            P(None, "mp", both),
            P(None, both),
            P(None, both, None, "mp"),
            P(None, "mp", both),
        ),
        check_vma=False,
    )
```

```python
import jax
import jax.numpy as jnp
from jax import lax
from jax.sharding import PartitionSpec as P


HEAD_DIM = 64
GROUP = 7
LANES = 128

epsilon = 1e-06
base_theta = 1000000.0


f32 = jnp.float32
bf16 = jnp.bfloat16


def rope_tables(block_locations, head_dim):
    half_dim = head_dim // 2
    inv_freq = base_theta ** (-(jnp.arange(half_dim, dtype=f32) * 2.0) / head_dim)
    angles = block_locations.astype(f32)[:, None] * inv_freq[None, :]
    angles = jnp.concatenate([angles, angles], axis=1)
    return (jnp.cos(angles), jnp.sin(angles))


def rotate(values, cosine_lookup, sine_lookup):
    half_dim = values.shape[-1] // 2
    view_shape = (values.shape[0],) + (1,) * (values.ndim - 2) + (values.shape[-1],)
    turned = jnp.concatenate([-values[..., half_dim:], values[..., :half_dim]], axis=-1)
    return values * cosine_lookup.reshape(view_shape) + turned * sine_lookup.reshape(view_shape)


def rms_forward(hidden, gain_vec):
    scale_rows = lax.rsqrt(jnp.mean(hidden * hidden, axis=-1, keepdims=True) + epsilon)
    normed = hidden * scale_rows
    return (normed, scale_rows, (normed * gain_vec.astype(f32)).astype(bf16))


def rms_backward(grad_out, normed, scale_rows, gain_vec):
    gain_grad = jnp.sum(grad_out * normed, axis=0)
    grad_normed = grad_out * gain_vec.astype(f32)
    grad_in = scale_rows * (
        grad_normed - normed * jnp.mean(grad_normed * normed, axis=-1, keepdims=True)
    )
    return (grad_in, gain_grad)


def after(value, *others):
    return lax.optimization_barrier((value,) + others)[0]


def dot_nt(a, b):
    return lax.dot_general(a, b, (((1,), (1,)), ((), ())), preferred_element_type=f32)


def dot_tn(a, b):
    return lax.dot_general(a, b, (((0,), (0,)), ((), ())), preferred_element_type=f32)


def dot_nn(a, b):
    return jnp.dot(a, b, preferred_element_type=f32)


def make_local(n_dp, n_ctx, n_mp):
    n_lo = 2
    n_hi = n_ctx // n_lo
    assert n_dp == 2 and n_mp == 2 and n_hi * n_lo == n_ctx
    pair = [(0, 1), (1, 0)]
    lo_pair = [(i, i ^ 1) for i in range(n_ctx)]

    def swap_dp(v):
        return lax.ppermute(v, "dp", pair)

    def swap_mp(v):
        return lax.ppermute(v, "mp", pair)

    def swap_lo(v):
        return lax.ppermute(v, "ctx", lo_pair)

    def swap_hi(v, mask):
        perm = [(h * n_lo + e, (h ^ mask) * n_lo + e) for h in range(n_hi) for e in range(n_lo)]
        return lax.ppermute(v, "ctx", perm)

    def exchange(v, axes):
        return lax.all_to_all(v, axes, 0, 0, tiled=True)

    def in_order(flag, own, other, axis=0):
        first = flag == 0
        return jnp.stack([jnp.where(first, own, other), jnp.where(first, other, own)], axis=axis)

    def flipped(flag, pairs):
        return jnp.where(flag == 0, pairs, pairs[:, ::-1])

    def pick(flag, two):
        first = flag == 0
        return jnp.where(first, two[0], two[1]), jnp.where(first, two[1], two[0])

    def by_mask(got, hi):
        got = jnp.stack(got)
        return jnp.stack(
            [
                lax.dynamic_index_in_dim(got, jnp.bitwise_xor(hi, j), 0, keepdims=False)
                for j in range(n_hi)
            ]
        )

    def relay_masks():
        masks, step = [], n_hi // 2
        while step:
            masks.append(step)
            step //= 2
        return masks

    def scatter_hi(parts, hi):
        total = lax.dynamic_index_in_dim(parts, hi, 0, keepdims=False).astype(f32)
        for k in range(1, n_hi):
            part = lax.dynamic_index_in_dim(parts, jnp.bitwise_xor(hi, k), 0, keepdims=False)
            total = total + swap_hi(part, k).astype(f32)
        return total

    def gather_rows(block, c, hi, lo, start=None):
        got = [block] + [swap_hi(block, k) for k in range(1, n_hi)]
        if start is not None:
            got = [after(g, start) for g in got]
        mine = by_mask(got, hi)
        both = in_order(lo, mine, swap_lo(mine), axis=1)
        return in_order(c, both, swap_dp(both))

    def scatter_rows(parts, c, hi, lo):
        keep, send = pick(c, parts)
        keep = keep + swap_dp(send.astype(bf16)).astype(f32)
        keep, send = pick(lo, (keep[:, 0], keep[:, 1]))
        keep = keep + swap_lo(send.astype(bf16)).astype(f32)
        return scatter_hi(keep.astype(bf16), hi)

    def gather_tokens(block):
        both = jnp.concatenate([block, swap_lo(block)], axis=0)
        return jnp.concatenate([both, swap_dp(both)], axis=0)

    def scatter_tokens(parts):
        half = parts.shape[0] // 2
        keep = parts[:half] + swap_dp(parts[half:].astype(bf16)).astype(f32)
        half = half // 2
        keep = keep[:half] + swap_lo(keep[half:].astype(bf16)).astype(f32)
        return sum_mp(keep)

    def sum_mp(part):
        part = part.astype(bf16)
        return part.astype(f32) + swap_mp(part).astype(f32)

    def local(
        inputs,
        positions,
        attn_gain,
        qkv_weight,
        qkv_bias,
        out_weight,
        ffn_gain,
        gate_up_weight,
        down_weight,
        cotangent,
    ):
        c = lax.axis_index("dp")
        ctx = lax.axis_index("ctx")
        hi, lo = ctx // n_lo, ctx % n_lo
        tokens = inputs.shape[1]
        model_width = inputs.shape[2]
        head_dim = HEAD_DIM
        group_size = GROUP
        score_scale = head_dim ** (-0.5)
        rows = qkv_weight.shape[1]
        units = down_weight.shape[1]
        splits = n_dp * n_lo
        piece = -(-units // (splits * LANES)) * LANES
        n_shards = n_dp * n_ctx

        seq_pos = positions[0]
        my_pos = lax.dynamic_slice_in_dim(seq_pos, ctx * tokens, tokens)
        hidden = inputs[0]

        w_q = qkv_weight[0]
        width_q = w_q.shape[1]
        gain_cols = -(-rows // LANES) * LANES
        bias_cols = qkv_bias.shape[2]
        extra = jnp.concatenate(
            [
                jnp.pad(attn_gain[0], (0, gain_cols - rows)),
                jnp.pad(ffn_gain[0], (0, gain_cols - rows)),
                jnp.pad(qkv_bias[0, 0], (0, width_q - 2 * gain_cols - bias_cols)),
            ]
        )[None]
        extra = jnp.pad(extra, ((0, 7), (0, 0)))
        block_q = jnp.concatenate([w_q, extra], axis=0)
        got_q = gather_rows(block_q, c, hi, lo).reshape(n_shards, rows + 8, width_q)
        w_qkv = got_q[:, :rows].reshape(model_width, width_q)
        side = got_q[:, rows]
        gain_attn = side[:, :rows].reshape(model_width)
        gain_ffn = side[:, gain_cols : gain_cols + rows].reshape(model_width)
        b_qkv = side[:, 2 * gain_cols : 2 * gain_cols + bias_cols].reshape(width_q)

        gate_up_weight, down_weight, cotangent, my_pos, hidden, all_pos = (
            lax.optimization_barrier(
                (gate_up_weight, down_weight, cotangent, my_pos, hidden, seq_pos, block_q)
            )[:6]
        )
        shards = [gate_up_weight[0, :, 0], gate_up_weight[0, :, 1], down_weight[0].T]
        shards = [jnp.pad(s, ((0, 0), (0, splits * piece - units))) for s in shards]
        groups = [
            jnp.concatenate([s[:, q * piece : (q + 1) * piece] for s in shards], axis=1)
            for q in range(splits)
        ]
        halves = [jnp.stack(groups[e * n_dp : (e + 1) * n_dp]) for e in range(n_lo)]
        keep, send = pick(lo, halves)
        cosine_lookup, sine_lookup = rope_tables(my_pos, head_dim)
        key_pos = flipped(lo, all_pos.reshape(n_hi, n_lo, tokens))
        step = n_hi // 2
        while step:
            key_pos = flipped(hi // step % 2, key_pos.reshape(-1, 2, step * n_lo * tokens))
            step //= 2
        key_pos = key_pos.reshape(n_hi, n_lo, tokens).swapaxes(0, 1).reshape(-1)
        row_pos = jnp.tile(my_pos, group_size)
        both = in_order(lo, keep, swap_lo(send))
        block_o = after(out_weight[0].T, block_q)
        grad_out = cotangent[0]
        grad_half = gather_tokens(after(grad_out.astype(bf16), both))
        keep, send = pick(c, (both[:, 0], both[:, 1]))
        plane = in_order(c, keep, swap_dp(send))

        normed_a, scale_a, attn_in = rms_forward(hidden, gain_attn)
        qkv_proj = dot_nn(attn_in, w_qkv) + b_qkv.astype(f32)
        qkv_proj = qkv_proj.reshape(tokens, group_size + 2, head_dim)
        query_heads = rotate(qkv_proj[:, :group_size], cosine_lookup, sine_lookup).astype(bf16)
        key_head = rotate(
            qkv_proj[:, group_size : group_size + 1], cosine_lookup, sine_lookup
        )[:, 0].astype(bf16)
        value_head = qkv_proj[:, group_size + 1].astype(bf16)
        query_rows = jnp.transpose(query_heads, (1, 0, 2)).reshape(group_size * tokens, head_dim)
        pair_kv = jnp.concatenate([key_head, value_head], axis=1)
        w_ot = gather_rows(block_o, c, hi, lo, pair_kv).reshape(model_width, -1)
        relayed = {0: after(plane, pair_kv)}
        for mask in relay_masks():
            for k in list(relayed):
                relayed[k ^ mask] = swap_hi(relayed[k], mask)
        w_ffn = by_mask([relayed[k] for k in range(n_hi)], hi)
        w_ffn = jnp.transpose(w_ffn, (1, 0, 2, 3, 4)).reshape(model_width, 3 * piece)
        w_gu, w_dt = w_ffn[:, : 2 * piece], w_ffn[:, 2 * piece :]
        pair_kv = jnp.concatenate([pair_kv] + [swap_hi(pair_kv, k) for k in range(1, n_hi)], axis=0)
        pair_kv = jnp.concatenate([pair_kv, swap_lo(pair_kv)], axis=0)
        key_all, value_all = pair_kv[:, :head_dim], pair_kv[:, head_dim:]
        allowed = key_pos[None, :] <= row_pos[:, None]
        scores = dot_nt(query_rows, key_all) * score_scale
        scores = jnp.where(allowed, scores, -1e30)
        row_max = jnp.max(scores, axis=1)
        weights_now = jnp.where(allowed, jnp.exp(scores - row_max[:, None]), 0.0)
        row_total = jnp.sum(weights_now, axis=1)
        row_accum = jnp.dot(
            weights_now,
            value_all.astype(f32),
            precision=lax.Precision.HIGHEST,
            preferred_element_type=f32,
        )
        log_total = row_max + jnp.log(row_total)
        attn_rows = (row_accum / row_total[:, None]).astype(bf16)
        attn_flat = jnp.transpose(
            attn_rows.reshape(group_size, tokens, head_dim), (1, 0, 2)
        ).reshape(tokens, group_size * head_dim)
        hidden_mid = hidden + sum_mp(dot_nt(attn_flat, w_ot))

        normed_f, scale_f, ffn_in = rms_forward(hidden_mid, gain_ffn)
        ffn_all = gather_tokens(ffn_in)
        gate_up_pre = dot_nn(ffn_all, w_gu)
        gate_pre, up_pre = gate_up_pre[:, :piece], gate_up_pre[:, piece:]
        grad_mixed = dot_nn(grad_half, w_dt)
        sigmoid_gate = jax.nn.sigmoid(gate_pre)
        silu_gate = gate_pre * sigmoid_gate
        mixed_units = (silu_gate * up_pre).astype(bf16)
        grad_up = grad_mixed * silu_gate
        grad_gate = grad_mixed * up_pre * (sigmoid_gate + silu_gate * (1.0 - sigmoid_gate))
        grad_pre = jnp.concatenate([grad_gate, grad_up], axis=1).astype(bf16)
        ffn_in_grad = scatter_tokens(dot_nt(grad_pre, w_gu))
        hidden_next = hidden_mid + scatter_tokens(dot_nt(mixed_units, w_dt))
        w_grad = jnp.concatenate(
            [dot_tn(ffn_all, grad_pre), dot_tn(grad_half, mixed_units)], axis=1
        ).astype(bf16)
        w_grad = w_grad.reshape(n_dp, n_hi, n_lo, rows, 3 * piece)
        w_grad = jnp.transpose(w_grad, (1, 0, 2, 3, 4))
        parts = [
            lax.dynamic_index_in_dim(w_grad, jnp.bitwise_xor(hi, k), 0, keepdims=False)
            for k in range(n_hi)
        ]
        sums = {k: [part] for k, part in enumerate(parts)}
        for mask in reversed(relay_masks()):
            for k in sorted(sums, reverse=True):
                if k & mask:
                    terms = sums.pop(k)
                    if len(terms) > 1:
                        terms = [sum(m.astype(f32) for m in terms).astype(bf16)]
                    sums[k ^ mask].append(swap_hi(terms[0], mask))

        back_ffn, gain_ffn_part = rms_backward(ffn_in_grad, normed_f, scale_f, gain_ffn)
        grad_mid = grad_out + back_ffn
        grad_mid_half = grad_mid.astype(bf16)
        grad_attn = dot_nn(grad_mid_half, w_ot).astype(bf16)
        out_part = dot_tn(grad_mid_half, attn_flat)
        grad_rows = jnp.transpose(
            grad_attn.reshape(tokens, group_size, head_dim), (1, 0, 2)
        ).reshape(group_size * tokens, head_dim)
        delta_rows = jnp.sum(grad_rows.astype(f32) * attn_rows.astype(f32), axis=1)
        probs = jnp.where(allowed, jnp.exp(scores - log_total[:, None]), 0.0)
        value_grad_all = dot_tn(probs.astype(bf16), grad_rows)
        grad_probs = dot_nt(grad_rows, value_all)
        grad_scores = (probs * (grad_probs - delta_rows[:, None])).astype(bf16)
        query_grad = dot_nn(grad_scores, key_all) * score_scale
        key_grad_all = dot_tn(grad_scores, query_rows) * score_scale
        kv_grad = jnp.concatenate([key_grad_all, value_grad_all], axis=1)
        kv_grad = kv_grad.reshape(n_lo, n_hi, tokens, 2 * head_dim)
        kv_grad = kv_grad[0] + swap_lo(kv_grad[1].astype(bf16)).astype(f32)
        kv_grad = kv_grad[0] + sum(
            swap_hi(kv_grad[k].astype(bf16), k).astype(f32) for k in range(1, n_hi)
        )
        key_grad, value_grad = kv_grad[:, :head_dim], kv_grad[:, head_dim:]
        query_grad = jnp.transpose(query_grad.reshape(group_size, tokens, head_dim), (1, 0, 2))
        query_grad = rotate(query_grad, cosine_lookup, -sine_lookup)
        key_grad = rotate(key_grad[:, None], cosine_lookup, -sine_lookup)
        grad_qkv = jnp.concatenate([query_grad, key_grad, value_grad[:, None]], axis=1).reshape(
            tokens, (group_size + 2) * head_dim
        )
        bias_part = jnp.sum(grad_qkv, axis=0)
        grad_qkv_half = grad_qkv.astype(bf16)
        attn_in_grad = sum_mp(dot_nt(grad_qkv_half, w_qkv))
        back_attn, gain_attn_part = rms_backward(attn_in_grad, normed_a, scale_a, gain_attn)
        input_grad = grad_mid + back_attn
        qkv_part = dot_tn(attn_in, grad_qkv_half)

        row_parts = jnp.concatenate([qkv_part, out_part], axis=1)
        row_sums = scatter_rows(row_parts.reshape(n_dp, n_hi, n_lo, rows, -1), c, hi, lo)
        qkv_sum, out_grad = row_sums[:, :width_q], row_sums[:, width_q:]
        side = jnp.stack(
            [
                jnp.pad(v.reshape(n_shards, -1), ((0, 0), (0, gain_cols - v.shape[0] // n_shards)))
                for v in (gain_attn_part, gain_ffn_part, bias_part)
            ],
            axis=1,
        )
        side = jnp.pad(side, ((0, 0), (0, 5), (0, 0)))
        side = jnp.sum(exchange(side, ("dp", "ctx")), axis=0)

        w_grad = sum(after(m, grad_qkv_half).astype(f32) for m in sums[0]).astype(bf16)
        keep, send = pick(c, w_grad)
        by_c = in_order(c, keep, swap_dp(send))
        keep, send = pick(lo, (by_c[:, 0], by_c[:, 1]))
        by_q = in_order(lo, keep, swap_lo(send)).reshape(splits, rows, 3 * piece).astype(f32)
        gate_grad, up_grad, down_grad = [
            jnp.concatenate(
                [by_q[q, :, e * piece : (e + 1) * piece] for q in range(splits)], axis=1
            )[:, :units]
            for e in range(3)
        ]
        return (
            hidden_next[None],
            input_grad[None],
            side[:1, :rows],
            qkv_sum[None],
            side[2:3, :bias_cols][None],
            out_grad.T[None],
            side[1:2, :rows],
            jnp.stack([gate_grad, up_grad], axis=1)[None],
            down_grad.T[None],
        )

    return local


def solution(mesh):
    both = ("dp", "ctx")
    body = make_local(mesh.shape["dp"], mesh.shape["ctx"], mesh.shape["mp"])

    return jax.shard_map(
        body,
        mesh=mesh,
        in_specs=(
            P("dp", "ctx", None),
            P("dp", None),
            P(None, both),
            P(None, both, "mp"),
            P(None, "mp", both),
            P(None, "mp", both),
            P(None, both),
            P(None, both, None, "mp"),
            P(None, "mp", both),
            P("dp", "ctx", None),
        ),
        out_specs=(
            P("dp", "ctx", None),
            P("dp", "ctx", None),
            P(None, both),
            P(None, both, "mp"),
            P(None, "mp", both),
            P(None, "mp", both),
            P(None, both),
            P(None, both, None, "mp"),
            P(None, "mp", both),
        ),
        check_vma=False,
    )
```

```python
import jax
import jax.numpy as jnp
from jax import lax
from jax.sharding import PartitionSpec as P


HEAD_DIM = 64
GROUP = 7
LANES = 128

epsilon = 1e-06
base_theta = 1000000.0


f32 = jnp.float32
bf16 = jnp.bfloat16


def rope_tables(block_locations, head_dim):
    half_dim = head_dim // 2
    inv_freq = base_theta ** (-(jnp.arange(half_dim, dtype=f32) * 2.0) / head_dim)
    angles = block_locations.astype(f32)[:, None] * inv_freq[None, :]
    angles = jnp.concatenate([angles, angles], axis=1)
    return (jnp.cos(angles), jnp.sin(angles))


def rotate(values, cosine_lookup, sine_lookup):
    half_dim = values.shape[-1] // 2
    view_shape = (values.shape[0],) + (1,) * (values.ndim - 2) + (values.shape[-1],)
    turned = jnp.concatenate([-values[..., half_dim:], values[..., :half_dim]], axis=-1)
    return values * cosine_lookup.reshape(view_shape) + turned * sine_lookup.reshape(view_shape)


def rms_forward(hidden, gain_vec):
    scale_rows = lax.rsqrt(jnp.mean(hidden * hidden, axis=-1, keepdims=True) + epsilon)
    normed = hidden * scale_rows
    return (normed, scale_rows, (normed * gain_vec.astype(f32)).astype(bf16))


def rms_backward(grad_out, normed, scale_rows, gain_vec):
    gain_grad = jnp.sum(grad_out * normed, axis=0)
    grad_normed = grad_out * gain_vec.astype(f32)
    grad_in = scale_rows * (
        grad_normed - normed * jnp.mean(grad_normed * normed, axis=-1, keepdims=True)
    )
    return (grad_in, gain_grad)


def after(value, *others):
    return lax.optimization_barrier((value,) + others)[0]


def summed(terms):
    if len(terms) == 1:
        return terms[0]
    return sum(m.astype(f32) for m in terms).astype(bf16)


def dot_nt(a, b):
    return lax.dot_general(a, b, (((1,), (1,)), ((), ())), preferred_element_type=f32)


def dot_tn(a, b):
    return lax.dot_general(a, b, (((0,), (0,)), ((), ())), preferred_element_type=f32)


def dot_nn(a, b):
    return jnp.dot(a, b, preferred_element_type=f32)


def make_local(n_dp, n_ctx, n_mp):
    n_lo = 2
    n_hi = n_ctx // n_lo
    assert n_dp == 2 and n_mp == 2 and n_hi * n_lo == n_ctx
    pair = [(0, 1), (1, 0)]
    lo_pair = [(i, i ^ 1) for i in range(n_ctx)]

    def swap_dp(v):
        return lax.ppermute(v, "dp", pair)

    def swap_mp(v):
        return lax.ppermute(v, "mp", pair)

    def swap_lo(v):
        return lax.ppermute(v, "ctx", lo_pair)

    def swap_hi(v, mask):
        perm = [(h * n_lo + e, (h ^ mask) * n_lo + e) for h in range(n_hi) for e in range(n_lo)]
        return lax.ppermute(v, "ctx", perm)

    def exchange(v, axes):
        return lax.all_to_all(v, axes, 0, 0, tiled=True)

    def in_order(flag, own, other, axis=0):
        first = flag == 0
        return jnp.stack([jnp.where(first, own, other), jnp.where(first, other, own)], axis=axis)

    def flipped(flag, pairs):
        return jnp.where(flag == 0, pairs, pairs[:, ::-1])

    def pick(flag, two):
        first = flag == 0
        return jnp.where(first, two[0], two[1]), jnp.where(first, two[1], two[0])

    def by_mask(got, hi):
        got = jnp.stack(got)
        return jnp.stack(
            [
                lax.dynamic_index_in_dim(got, jnp.bitwise_xor(hi, j), 0, keepdims=False)
                for j in range(n_hi)
            ]
        )

    def relay_masks():
        masks, step = [], n_hi // 2
        while step:
            masks.append(step)
            step //= 2
        return masks

    def scatter_hi(parts, hi):
        total = lax.dynamic_index_in_dim(parts, hi, 0, keepdims=False).astype(f32)
        for k in range(1, n_hi):
            part = lax.dynamic_index_in_dim(parts, jnp.bitwise_xor(hi, k), 0, keepdims=False)
            part = swap_hi(part, k)
            total = total + part.astype(f32)
        return total

    def gather_rows(block, c, hi, lo, start=None):
        got = [block] + [swap_hi(block, k) for k in range(1, n_hi)]
        if start is not None:
            got = [after(g, start) for g in got]
        mine = by_mask(got, hi)
        both = in_order(lo, mine, swap_lo(mine), axis=1)
        return in_order(c, both, swap_dp(both))

    def scatter_near(parts, c, lo):
        keep, send = pick(c, parts)
        keep = keep + swap_dp(send.astype(bf16)).astype(f32)
        keep, send = pick(lo, (keep[:, 0], keep[:, 1]))
        return (keep + swap_lo(send.astype(bf16)).astype(f32)).astype(bf16)

    def gather_tokens(block):
        both = jnp.concatenate([block, swap_lo(block)], axis=0)
        return jnp.concatenate([both, swap_dp(both)], axis=0)

    def scatter_tokens(parts):
        half = parts.shape[0] // 2
        keep = parts[:half] + swap_dp(parts[half:].astype(bf16)).astype(f32)
        half = half // 2
        keep = keep[:half] + swap_lo(keep[half:].astype(bf16)).astype(f32)
        return sum_mp(keep)

    def sum_mp(part):
        part = part.astype(bf16)
        return part.astype(f32) + swap_mp(part).astype(f32)

    def local(
        inputs,
        positions,
        attn_gain,
        qkv_weight,
        qkv_bias,
        out_weight,
        ffn_gain,
        gate_up_weight,
        down_weight,
        cotangent,
    ):
        c = lax.axis_index("dp")
        ctx = lax.axis_index("ctx")
        hi, lo = ctx // n_lo, ctx % n_lo
        tokens = inputs.shape[1]
        model_width = inputs.shape[2]
        head_dim = HEAD_DIM
        group_size = GROUP
        score_scale = head_dim ** (-0.5)
        rows = qkv_weight.shape[1]
        units = down_weight.shape[1]
        splits = n_dp * n_lo
        piece = -(-units // (splits * LANES)) * LANES
        n_shards = n_dp * n_ctx

        seq_pos = positions[0]
        my_pos = lax.dynamic_slice_in_dim(seq_pos, ctx * tokens, tokens)
        hidden = inputs[0]

        w_q = qkv_weight[0]
        width_q = w_q.shape[1]
        gain_cols = -(-rows // LANES) * LANES
        bias_cols = qkv_bias.shape[2]
        extra = jnp.concatenate(
            [
                jnp.pad(attn_gain[0], (0, gain_cols - rows)),
                jnp.pad(ffn_gain[0], (0, gain_cols - rows)),
                jnp.pad(qkv_bias[0, 0], (0, width_q - 2 * gain_cols - bias_cols)),
            ]
        )[None]
        extra = jnp.pad(extra, ((0, 7), (0, 0)))
        block_q = jnp.concatenate([w_q, extra], axis=0)
        got_q = gather_rows(block_q, c, hi, lo).reshape(n_shards, rows + 8, width_q)
        w_qkv = got_q[:, :rows].reshape(model_width, width_q)
        side = got_q[:, rows]
        gain_attn = side[:, :rows].reshape(model_width)
        gain_ffn = side[:, gain_cols : gain_cols + rows].reshape(model_width)
        b_qkv = side[:, 2 * gain_cols : 2 * gain_cols + bias_cols].reshape(width_q)

        gate_up_weight, down_weight, cotangent, my_pos, hidden, all_pos = (
            lax.optimization_barrier(
                (gate_up_weight, down_weight, cotangent, my_pos, hidden, seq_pos, block_q)
            )[:6]
        )
        shards = [gate_up_weight[0, :, 0], gate_up_weight[0, :, 1], down_weight[0].T]
        shards = [jnp.pad(s, ((0, 0), (0, splits * piece - units))) for s in shards]
        groups = [
            jnp.concatenate([s[:, q * piece : (q + 1) * piece] for s in shards], axis=1)
            for q in range(splits)
        ]
        halves = [jnp.stack(groups[e * n_dp : (e + 1) * n_dp]) for e in range(n_lo)]
        keep, send = pick(lo, halves)
        cosine_lookup, sine_lookup = rope_tables(my_pos, head_dim)
        key_pos = flipped(lo, all_pos.reshape(n_hi, n_lo, tokens))
        step = n_hi // 2
        while step:
            key_pos = flipped(hi // step % 2, key_pos.reshape(-1, 2, step * n_lo * tokens))
            step //= 2
        key_pos = key_pos.reshape(n_hi, n_lo, tokens).swapaxes(0, 1).reshape(-1)
        row_pos = jnp.tile(my_pos, group_size)
        both = in_order(lo, keep, swap_lo(send))
        block_o = after(out_weight[0].T, block_q)
        grad_out = cotangent[0]
        grad_half = gather_tokens(after(grad_out.astype(bf16), both))
        keep, send = pick(c, (both[:, 0], both[:, 1]))
        plane = in_order(c, keep, swap_dp(send))

        normed_a, scale_a, attn_in = rms_forward(hidden, gain_attn)
        qkv_proj = dot_nn(attn_in, w_qkv) + b_qkv.astype(f32)
        qkv_proj = qkv_proj.reshape(tokens, group_size + 2, head_dim)
        query_heads = rotate(qkv_proj[:, :group_size], cosine_lookup, sine_lookup).astype(bf16)
        key_head = rotate(
            qkv_proj[:, group_size : group_size + 1], cosine_lookup, sine_lookup
        )[:, 0].astype(bf16)
        value_head = qkv_proj[:, group_size + 1].astype(bf16)
        query_rows = jnp.transpose(query_heads, (1, 0, 2)).reshape(group_size * tokens, head_dim)
        pair_kv = jnp.concatenate([key_head, value_head], axis=1)
        w_ot = gather_rows(block_o, c, hi, lo, pair_kv).reshape(model_width, -1)
        plane = after(plane, pair_kv)
        cut = 2 * piece
        relays = {}
        for part, block in (("gu", plane[..., :cut]), ("d", plane[..., cut:])):
            got = {0: block}
            for mask in relay_masks():
                for k in list(got):
                    got[k ^ mask] = swap_hi(got[k], mask)
            got = by_mask([got[k] for k in range(n_hi)], hi)
            relays[part] = jnp.transpose(got, (1, 0, 2, 3, 4)).reshape(model_width, -1)
        w_gu, w_dt = relays["gu"], relays["d"]
        pair_kv = jnp.concatenate([pair_kv] + [swap_hi(pair_kv, k) for k in range(1, n_hi)], axis=0)
        pair_kv = jnp.concatenate([pair_kv, swap_lo(pair_kv)], axis=0)
        key_all, value_all = pair_kv[:, :head_dim], pair_kv[:, head_dim:]
        allowed = key_pos[None, :] <= row_pos[:, None]
        scores = dot_nt(query_rows, key_all) * score_scale
        scores = jnp.where(allowed, scores, -1e30)
        row_max = jnp.max(scores, axis=1)
        weights_now = jnp.where(allowed, jnp.exp(scores - row_max[:, None]), 0.0)
        row_total = jnp.sum(weights_now, axis=1)
        row_accum = jnp.dot(
            weights_now,
            value_all.astype(f32),
            precision=lax.Precision.HIGHEST,
            preferred_element_type=f32,
        )
        log_total = row_max + jnp.log(row_total)
        attn_rows = (row_accum / row_total[:, None]).astype(bf16)
        attn_flat = jnp.transpose(
            attn_rows.reshape(group_size, tokens, head_dim), (1, 0, 2)
        ).reshape(tokens, group_size * head_dim)
        hidden_mid = hidden + sum_mp(dot_nt(attn_flat, w_ot))

        normed_f, scale_f, ffn_in = rms_forward(hidden_mid, gain_ffn)
        ffn_all = gather_tokens(ffn_in)
        gate_up_pre = dot_nn(ffn_all, w_gu)
        gate_pre, up_pre = gate_up_pre[:, :piece], gate_up_pre[:, piece:]
        grad_mixed = dot_nn(grad_half, w_dt)
        sigmoid_gate = jax.nn.sigmoid(gate_pre)
        silu_gate = gate_pre * sigmoid_gate
        mixed_units = (silu_gate * up_pre).astype(bf16)
        grad_up = grad_mixed * silu_gate
        grad_gate = grad_mixed * up_pre * (sigmoid_gate + silu_gate * (1.0 - sigmoid_gate))
        grad_pre = jnp.concatenate([grad_gate, grad_up], axis=1).astype(bf16)
        ffn_in_grad = scatter_tokens(dot_nt(grad_pre, w_gu))
        hidden_next = hidden_mid + scatter_tokens(dot_nt(mixed_units, w_dt))
        far = n_hi // 2
        own_sum, far_sum = {}, {}
        for part, full in (
            ("gu", dot_tn(ffn_all, grad_pre)),
            ("d", dot_tn(grad_half, mixed_units)),
        ):
            full = full.astype(bf16).reshape(n_dp, n_hi, n_lo, rows, -1)
            full = jnp.transpose(full, (1, 0, 2, 3, 4))
            sums = {
                k: [lax.dynamic_index_in_dim(full, jnp.bitwise_xor(hi, k), 0, keepdims=False)]
                for k in range(n_hi)
            }
            for mask in reversed(relay_masks()[1:]):
                for k in sorted(sums, reverse=True):
                    if k & mask:
                        arrived = swap_hi(summed(sums.pop(k)), mask)
                        sums[k ^ mask].append(arrived)
            own_sum[part], far_sum[part] = sums[0], sums[far]
        far_sum["gu"] = swap_hi(summed(far_sum["gu"]), far)

        back_ffn, gain_ffn_part = rms_backward(ffn_in_grad, normed_f, scale_f, gain_ffn)
        grad_mid = grad_out + back_ffn
        grad_mid_half = grad_mid.astype(bf16)
        grad_attn = dot_nn(grad_mid_half, w_ot).astype(bf16)
        out_part = dot_tn(grad_mid_half, attn_flat)
        out_near = scatter_near(out_part.reshape(n_dp, n_hi, n_lo, rows, -1), c, lo)
        grad_rows = jnp.transpose(
            grad_attn.reshape(tokens, group_size, head_dim), (1, 0, 2)
        ).reshape(group_size * tokens, head_dim)
        delta_rows = jnp.sum(grad_rows.astype(f32) * attn_rows.astype(f32), axis=1)
        probs = jnp.where(allowed, jnp.exp(scores - log_total[:, None]), 0.0)
        value_grad_all = dot_tn(probs.astype(bf16), grad_rows)
        grad_probs = dot_nt(grad_rows, value_all)
        grad_scores = (probs * (grad_probs - delta_rows[:, None])).astype(bf16)
        query_grad = dot_nn(grad_scores, key_all) * score_scale
        key_grad_all = dot_tn(grad_scores, query_rows) * score_scale
        kv_grad = jnp.concatenate([key_grad_all, value_grad_all], axis=1)
        far_sum["d"] = [after(m, kv_grad) for m in far_sum["d"]]
        far_sum["d"] = swap_hi(summed(far_sum["d"]), far)
        kv_grad = kv_grad.reshape(n_lo, n_hi, tokens, 2 * head_dim)
        kv_grad = kv_grad[0] + swap_lo(kv_grad[1].astype(bf16)).astype(f32)
        kv_grad = kv_grad[0] + sum(
            swap_hi(kv_grad[k].astype(bf16), k).astype(f32) for k in range(1, n_hi)
        )
        key_grad, value_grad = kv_grad[:, :head_dim], kv_grad[:, head_dim:]
        query_grad = jnp.transpose(query_grad.reshape(group_size, tokens, head_dim), (1, 0, 2))
        query_grad = rotate(query_grad, cosine_lookup, -sine_lookup)
        key_grad = rotate(key_grad[:, None], cosine_lookup, -sine_lookup)
        grad_qkv = jnp.concatenate([query_grad, key_grad, value_grad[:, None]], axis=1).reshape(
            tokens, (group_size + 2) * head_dim
        )
        bias_part = jnp.sum(grad_qkv, axis=0)
        grad_qkv_half = grad_qkv.astype(bf16)
        attn_in_grad = sum_mp(dot_nt(grad_qkv_half, w_qkv))
        back_attn, gain_attn_part = rms_backward(attn_in_grad, normed_a, scale_a, gain_attn)
        input_grad = grad_mid + back_attn
        qkv_part = dot_tn(attn_in, grad_qkv_half)

        qkv_near = scatter_near(qkv_part.reshape(n_dp, n_hi, n_lo, rows, -1), c, lo)
        row_sums = scatter_hi(jnp.concatenate([qkv_near, out_near], axis=-1), hi)
        qkv_sum, out_grad = row_sums[:, :width_q], row_sums[:, width_q:]
        side = jnp.stack(
            [
                jnp.pad(v.reshape(n_shards, -1), ((0, 0), (0, gain_cols - v.shape[0] // n_shards)))
                for v in (gain_attn_part, gain_ffn_part, bias_part)
            ],
            axis=1,
        )
        w_grad = jnp.concatenate(
            [
                sum(after(m, qkv_near).astype(f32) for m in own_sum[part] + [far_sum[part]])
                for part in ("gu", "d")
            ],
            axis=-1,
        ).astype(bf16)
        keep, send = pick(c, w_grad)
        by_c = in_order(c, keep, swap_dp(send))
        keep, send = pick(lo, (by_c[:, 0], by_c[:, 1]))
        side = jnp.pad(after(side, send), ((0, 0), (0, 5), (0, 0)))
        side = jnp.sum(exchange(side, ("dp", "ctx")), axis=0)
        by_q = in_order(lo, keep, swap_lo(send)).reshape(splits, rows, 3 * piece).astype(f32)
        gate_grad, up_grad, down_grad = [
            jnp.concatenate(
                [by_q[q, :, e * piece : (e + 1) * piece] for q in range(splits)], axis=1
            )[:, :units]
            for e in range(3)
        ]
        return (
            hidden_next[None],
            input_grad[None],
            side[:1, :rows],
            qkv_sum[None],
            side[2:3, :bias_cols][None],
            out_grad.T[None],
            side[1:2, :rows],
            jnp.stack([gate_grad, up_grad], axis=1)[None],
            down_grad.T[None],
        )

    return local


def solution(mesh):
    both = ("dp", "ctx")
    body = make_local(mesh.shape["dp"], mesh.shape["ctx"], mesh.shape["mp"])

    return jax.shard_map(
        body,
        mesh=mesh,
        in_specs=(
            P("dp", "ctx", None),
            P("dp", None),
            P(None, both),
            P(None, both, "mp"),
            P(None, "mp", both),
            P(None, "mp", both),
            P(None, both),
            P(None, both, None, "mp"),
            P(None, "mp", both),
            P("dp", "ctx", None),
        ),
        out_specs=(
            P("dp", "ctx", None),
            P("dp", "ctx", None),
            P(None, both),
            P(None, both, "mp"),
            P(None, "mp", both),
            P(None, "mp", both),
            P(None, both),
            P(None, both, None, "mp"),
            P(None, "mp", both),
        ),
        check_vma=False,
    )
```

```python
import jax
import jax.numpy as jnp
from jax import lax
from jax.sharding import PartitionSpec as P


HEAD_DIM = 64
GROUP = 7
LANES = 128

epsilon = 1e-06
base_theta = 1000000.0


f32 = jnp.float32
bf16 = jnp.bfloat16


def rope_tables(block_locations, head_dim):
    half_dim = head_dim // 2
    inv_freq = base_theta ** (-(jnp.arange(half_dim, dtype=f32) * 2.0) / head_dim)
    angles = block_locations.astype(f32)[:, None] * inv_freq[None, :]
    angles = jnp.concatenate([angles, angles], axis=1)
    return (jnp.cos(angles), jnp.sin(angles))


def rotate(values, cosine_lookup, sine_lookup):
    half_dim = values.shape[-1] // 2
    view_shape = (values.shape[0],) + (1,) * (values.ndim - 2) + (values.shape[-1],)
    turned = jnp.concatenate([-values[..., half_dim:], values[..., :half_dim]], axis=-1)
    return values * cosine_lookup.reshape(view_shape) + turned * sine_lookup.reshape(view_shape)


def rms_forward(hidden, gain_vec):
    scale_rows = lax.rsqrt(jnp.mean(hidden * hidden, axis=-1, keepdims=True) + epsilon)
    normed = hidden * scale_rows
    return (normed, scale_rows, (normed * gain_vec.astype(f32)).astype(bf16))


def rms_backward(grad_out, normed, scale_rows, gain_vec):
    gain_grad = jnp.sum(grad_out * normed, axis=0)
    grad_normed = grad_out * gain_vec.astype(f32)
    grad_in = scale_rows * (
        grad_normed - normed * jnp.mean(grad_normed * normed, axis=-1, keepdims=True)
    )
    return (grad_in, gain_grad)


def after(value, *others):
    return lax.optimization_barrier((value,) + others)[0]


def summed(terms):
    if len(terms) == 1:
        return terms[0]
    return sum(m.astype(f32) for m in terms).astype(bf16)


def dot_nt(a, b):
    return lax.dot_general(a, b, (((1,), (1,)), ((), ())), preferred_element_type=f32)


def dot_tn(a, b):
    return lax.dot_general(a, b, (((0,), (0,)), ((), ())), preferred_element_type=f32)


def dot_nn(a, b):
    return jnp.dot(a, b, preferred_element_type=f32)


def make_local(n_dp, n_ctx, n_mp):
    n_lo = 2
    n_hi = n_ctx // n_lo
    assert n_dp == 2 and n_mp == 2 and n_hi * n_lo == n_ctx
    pair = [(0, 1), (1, 0)]
    lo_pair = [(i, i ^ 1) for i in range(n_ctx)]

    def swap_dp(v):
        return lax.ppermute(v, "dp", pair)

    def swap_mp(v):
        return lax.ppermute(v, "mp", pair)

    def swap_lo(v):
        return lax.ppermute(v, "ctx", lo_pair)

    def swap_hi(v, mask):
        perm = [(h * n_lo + e, (h ^ mask) * n_lo + e) for h in range(n_hi) for e in range(n_lo)]
        return lax.ppermute(v, "ctx", perm)

    def exchange(v, axes):
        return lax.all_to_all(v, axes, 0, 0, tiled=True)

    def in_order(flag, own, other, axis=0):
        first = flag == 0
        return jnp.stack([jnp.where(first, own, other), jnp.where(first, other, own)], axis=axis)

    def flipped(flag, pairs):
        return jnp.where(flag == 0, pairs, pairs[:, ::-1])

    def pick(flag, two):
        first = flag == 0
        return jnp.where(first, two[0], two[1]), jnp.where(first, two[1], two[0])

    def by_mask(got, hi):
        got = jnp.stack(got)
        return jnp.stack(
            [
                lax.dynamic_index_in_dim(got, jnp.bitwise_xor(hi, j), 0, keepdims=False)
                for j in range(n_hi)
            ]
        )

    def relay_masks():
        masks, step = [], n_hi // 2
        while step:
            masks.append(step)
            step //= 2
        return masks

    def scatter_hi(parts, hi):
        total = lax.dynamic_index_in_dim(parts, hi, 0, keepdims=False).astype(f32)
        for k in range(1, n_hi):
            part = lax.dynamic_index_in_dim(parts, jnp.bitwise_xor(hi, k), 0, keepdims=False)
            part = swap_hi(part, k)
            total = total + part.astype(f32)
        return total

    def gather_rows(block, c, hi, lo, start=None):
        got = [block] + [swap_hi(block, k) for k in range(1, n_hi)]
        if start is not None:
            got = [after(g, start) for g in got]
        mine = by_mask(got, hi)
        both = in_order(lo, mine, swap_lo(mine), axis=1)
        return in_order(c, both, swap_dp(both))

    def scatter_near(parts, c, lo):
        keep, sent = pick(c, parts.astype(bf16))
        keep = keep.astype(f32) + swap_dp(sent).astype(f32)
        keep, send = pick(lo, (keep[:, 0], keep[:, 1]))
        near = keep + swap_lo(send.astype(bf16)).astype(f32)
        return near.astype(bf16), sent

    def gather_tokens(block):
        both = jnp.concatenate([block, swap_lo(block)], axis=0)
        return jnp.concatenate([both, swap_dp(both)], axis=0)

    def scatter_tokens(parts):
        half = parts.shape[0] // 2
        keep = parts[:half] + swap_dp(parts[half:].astype(bf16)).astype(f32)
        half = half // 2
        keep = keep[:half] + swap_lo(keep[half:].astype(bf16)).astype(f32)
        return sum_mp(keep)

    def sum_mp(part):
        part = part.astype(bf16)
        return part.astype(f32) + swap_mp(part).astype(f32)

    def local(
        inputs,
        positions,
        attn_gain,
        qkv_weight,
        qkv_bias,
        out_weight,
        ffn_gain,
        gate_up_weight,
        down_weight,
        cotangent,
    ):
        c = lax.axis_index("dp")
        ctx = lax.axis_index("ctx")
        hi, lo = ctx // n_lo, ctx % n_lo
        tokens = inputs.shape[1]
        model_width = inputs.shape[2]
        head_dim = HEAD_DIM
        group_size = GROUP
        score_scale = head_dim ** (-0.5)
        rows = qkv_weight.shape[1]
        units = down_weight.shape[1]
        splits = n_dp * n_lo
        piece = -(-units // (splits * LANES)) * LANES
        n_shards = n_dp * n_ctx

        seq_pos = positions[0]
        my_pos = lax.dynamic_slice_in_dim(seq_pos, ctx * tokens, tokens)
        hidden = inputs[0]

        w_q = qkv_weight[0]
        width_q = w_q.shape[1]
        gain_cols = -(-rows // LANES) * LANES
        bias_cols = qkv_bias.shape[2]
        extra = jnp.concatenate(
            [
                jnp.pad(attn_gain[0], (0, gain_cols - rows)),
                jnp.pad(ffn_gain[0], (0, gain_cols - rows)),
                jnp.pad(qkv_bias[0, 0], (0, width_q - 2 * gain_cols - bias_cols)),
            ]
        )[None]
        extra = jnp.pad(extra, ((0, 7), (0, 0)))
        block_q = jnp.concatenate([w_q, extra], axis=0)
        got_q = gather_rows(block_q, c, hi, lo).reshape(n_shards, rows + 8, width_q)
        w_qkv = got_q[:, :rows].reshape(model_width, width_q)
        side = got_q[:, rows]
        gain_attn = side[:, :rows].reshape(model_width)
        gain_ffn = side[:, gain_cols : gain_cols + rows].reshape(model_width)
        b_qkv = side[:, 2 * gain_cols : 2 * gain_cols + bias_cols].reshape(width_q)

        gate_up_weight, down_weight, cotangent, my_pos, hidden, all_pos = (
            lax.optimization_barrier(
                (gate_up_weight, down_weight, cotangent, my_pos, hidden, seq_pos, block_q)
            )[:6]
        )
        shards = [gate_up_weight[0, :, 0], gate_up_weight[0, :, 1], down_weight[0].T]
        shards = [jnp.pad(s, ((0, 0), (0, splits * piece - units))) for s in shards]
        groups = [
            jnp.concatenate([s[:, q * piece : (q + 1) * piece] for s in shards], axis=1)
            for q in range(splits)
        ]
        halves = [jnp.stack(groups[e * n_dp : (e + 1) * n_dp]) for e in range(n_lo)]
        keep, send = pick(lo, halves)
        cosine_lookup, sine_lookup = rope_tables(my_pos, head_dim)
        key_pos = flipped(lo, all_pos.reshape(n_hi, n_lo, tokens))
        step = n_hi // 2
        while step:
            key_pos = flipped(hi // step % 2, key_pos.reshape(-1, 2, step * n_lo * tokens))
            step //= 2
        key_pos = key_pos.reshape(n_hi, n_lo, tokens).swapaxes(0, 1).reshape(-1)
        row_pos = jnp.tile(my_pos, group_size)
        both = in_order(lo, keep, swap_lo(send))
        block_o = after(out_weight[0].T, block_q)
        grad_out = cotangent[0]
        keep, send = pick(c, (both[:, 0], both[:, 1]))
        plane = in_order(c, keep, swap_dp(send))

        normed_a, scale_a, attn_in = rms_forward(hidden, gain_attn)
        attn_in = lax.optimization_barrier(attn_in)
        qkv_proj = dot_nn(attn_in, w_qkv) + b_qkv.astype(f32)
        qkv_proj = qkv_proj.reshape(tokens, group_size + 2, head_dim)
        query_heads = rotate(qkv_proj[:, :group_size], cosine_lookup, sine_lookup).astype(bf16)
        key_head = rotate(
            qkv_proj[:, group_size : group_size + 1], cosine_lookup, sine_lookup
        )[:, 0].astype(bf16)
        value_head = qkv_proj[:, group_size + 1].astype(bf16)
        query_rows = jnp.transpose(query_heads, (1, 0, 2)).reshape(group_size * tokens, head_dim)
        pair_kv = jnp.concatenate([key_head, value_head], axis=1)
        grad_half = gather_tokens(after(grad_out.astype(bf16), pair_kv))
        w_ot = gather_rows(block_o, c, hi, lo, pair_kv).reshape(model_width, -1)
        plane = after(plane, pair_kv)
        cut = 2 * piece
        relays = {}
        for part, block in (("gu", plane[..., :cut]), ("d", plane[..., cut:])):
            got = {0: block}
            for mask in relay_masks():
                for k in list(got):
                    got[k ^ mask] = swap_hi(got[k], mask)
            got = by_mask([got[k] for k in range(n_hi)], hi)
            relays[part] = jnp.transpose(got, (1, 0, 2, 3, 4)).reshape(model_width, -1)
        w_gu, w_dt = relays["gu"], relays["d"]
        pair_kv = jnp.concatenate([pair_kv] + [swap_hi(pair_kv, k) for k in range(1, n_hi)], axis=0)
        pair_kv = jnp.concatenate([pair_kv, swap_lo(pair_kv)], axis=0)
        key_all, value_all = pair_kv[:, :head_dim], pair_kv[:, head_dim:]
        allowed = key_pos[None, :] <= row_pos[:, None]
        scores = dot_nt(query_rows, key_all) * score_scale
        scores = jnp.where(allowed, scores, -1e30)
        row_max = jnp.max(scores, axis=1)
        weights_now = jnp.where(allowed, jnp.exp(scores - row_max[:, None]), 0.0)
        row_total = jnp.sum(weights_now, axis=1)
        row_accum = jnp.dot(
            weights_now,
            value_all.astype(f32),
            precision=lax.Precision.HIGHEST,
            preferred_element_type=f32,
        )
        log_total = row_max + jnp.log(row_total)
        attn_rows = (row_accum / row_total[:, None]).astype(bf16)
        attn_flat = jnp.transpose(
            attn_rows.reshape(group_size, tokens, head_dim), (1, 0, 2)
        ).reshape(tokens, group_size * head_dim)
        hidden_mid = hidden + sum_mp(dot_nt(attn_flat, w_ot))

        normed_f, scale_f, ffn_in = rms_forward(hidden_mid, gain_ffn)
        ffn_all = gather_tokens(ffn_in)
        gate_up_pre = dot_nn(ffn_all, w_gu)
        gate_pre, up_pre = gate_up_pre[:, :piece], gate_up_pre[:, piece:]
        grad_mixed = dot_nn(grad_half, w_dt)
        sigmoid_gate = jax.nn.sigmoid(gate_pre)
        silu_gate = gate_pre * sigmoid_gate
        mixed_units = (silu_gate * up_pre).astype(bf16)
        grad_up = grad_mixed * silu_gate
        grad_gate = grad_mixed * up_pre * (sigmoid_gate + silu_gate * (1.0 - sigmoid_gate))
        grad_pre = jnp.concatenate([grad_gate, grad_up], axis=1).astype(bf16)
        ffn_in_grad = scatter_tokens(dot_nt(grad_pre, w_gu))
        hidden_next = hidden_mid + scatter_tokens(dot_nt(mixed_units, w_dt))
        far = n_hi // 2
        own_sum, far_sum = {}, {}
        for part, full in (
            ("gu", dot_tn(ffn_all, grad_pre)),
            ("d", dot_tn(grad_half, mixed_units)),
        ):
            full = full.astype(bf16).reshape(n_dp, n_hi, n_lo, rows, -1)
            full = jnp.transpose(full, (1, 0, 2, 3, 4))
            sums = {
                k: [lax.dynamic_index_in_dim(full, jnp.bitwise_xor(hi, k), 0, keepdims=False)]
                for k in range(n_hi)
            }
            for mask in reversed(relay_masks()[1:]):
                for k in sorted(sums, reverse=True):
                    if k & mask:
                        arrived = swap_hi(summed(sums.pop(k)), mask)
                        sums[k ^ mask].append(arrived)
            own_sum[part], far_sum[part] = sums[0], sums[far]
        far_sum["gu"] = swap_hi(summed(far_sum["gu"]), far)

        back_ffn, gain_ffn_part = rms_backward(ffn_in_grad, normed_f, scale_f, gain_ffn)
        grad_mid = grad_out + back_ffn
        grad_mid_half = grad_mid.astype(bf16)
        grad_attn = dot_nn(grad_mid_half, w_ot).astype(bf16)
        out_part = dot_tn(grad_mid_half, attn_flat)
        out_near, _ = scatter_near(out_part.reshape(n_dp, n_hi, n_lo, rows, -1), c, lo)
        grad_rows = jnp.transpose(
            grad_attn.reshape(tokens, group_size, head_dim), (1, 0, 2)
        ).reshape(group_size * tokens, head_dim)
        delta_rows = jnp.sum(grad_rows.astype(f32) * attn_rows.astype(f32), axis=1)
        probs = jnp.where(allowed, jnp.exp(scores - log_total[:, None]), 0.0)
        value_grad_all = dot_tn(probs.astype(bf16), grad_rows)
        grad_probs = dot_nt(grad_rows, value_all)
        grad_scores = (probs * (grad_probs - delta_rows[:, None])).astype(bf16)
        query_grad = dot_nn(grad_scores, key_all) * score_scale
        key_grad_all = dot_tn(grad_scores, query_rows) * score_scale
        kv_grad = jnp.concatenate([key_grad_all, value_grad_all], axis=1)
        far_sum["d"] = [after(m, kv_grad) for m in far_sum["d"]]
        far_sum["d"] = swap_hi(summed(far_sum["d"]), far)
        kv_grad = kv_grad.reshape(n_lo, n_hi, tokens, 2 * head_dim)
        kv_grad = kv_grad[0] + swap_lo(kv_grad[1].astype(bf16)).astype(f32)
        arrived = [swap_hi(kv_grad[k].astype(bf16), k) for k in range(1, n_hi)]
        kv_grad = kv_grad[0] + sum(m.astype(f32) for m in arrived)
        key_grad, value_grad = kv_grad[:, :head_dim], kv_grad[:, head_dim:]
        query_grad = jnp.transpose(query_grad.reshape(group_size, tokens, head_dim), (1, 0, 2))
        query_grad = rotate(query_grad, cosine_lookup, -sine_lookup)
        key_grad = rotate(key_grad[:, None], cosine_lookup, -sine_lookup)
        grad_qkv = jnp.concatenate([query_grad, key_grad, value_grad[:, None]], axis=1).reshape(
            tokens, (group_size + 2) * head_dim
        )
        bias_part = jnp.sum(grad_qkv, axis=0)
        grad_qkv_half = grad_qkv.astype(bf16)
        attn_in_grad = sum_mp(dot_nt(grad_qkv_half, w_qkv))
        back_attn, gain_attn_part = rms_backward(attn_in_grad, normed_a, scale_a, gain_attn)
        input_grad = grad_mid + back_attn
        qkv_part = dot_tn(attn_in, grad_qkv_half)

        qkv_near, qkv_sent = scatter_near(qkv_part.reshape(n_dp, n_hi, n_lo, rows, -1), c, lo)
        row_sums = scatter_hi(jnp.concatenate([qkv_near, out_near], axis=-1), hi)
        qkv_sum, out_grad = row_sums[:, :width_q], row_sums[:, width_q:]
        side = jnp.stack(
            [
                jnp.pad(v.reshape(n_shards, -1), ((0, 0), (0, gain_cols - v.shape[0] // n_shards)))
                for v in (gain_attn_part, gain_ffn_part, bias_part)
            ],
            axis=1,
        )
        side = jnp.pad(side, ((0, 0), (0, 5), (0, 0)))
        side = jnp.sum(after(exchange(side, ("dp", "ctx")), row_sums), axis=0)
        by_q = {}
        for part, tie in (("gu", qkv_sent), ("d", qkv_near)):
            terms = own_sum[part] + [far_sum[part]]
            w_grad = sum(after(m, tie).astype(f32) for m in terms).astype(bf16)
            keep, send = pick(c, w_grad)
            by_c = in_order(c, keep, swap_dp(send))
            keep, send = pick(lo, (by_c[:, 0], by_c[:, 1]))
            whole = in_order(lo, keep, swap_lo(send))
            by_q[part] = whole.reshape(splits, rows, -1).astype(f32)

        def units_of(part, e):
            cols = [by_q[part][q, :, e * piece : (e + 1) * piece] for q in range(splits)]
            return jnp.concatenate(cols, axis=1)[:, :units]

        gate_grad, up_grad, down_grad = units_of("gu", 0), units_of("gu", 1), units_of("d", 0)
        return (
            hidden_next[None],
            input_grad[None],
            side[:1, :rows],
            qkv_sum[None],
            side[2:3, :bias_cols][None],
            out_grad.T[None],
            side[1:2, :rows],
            jnp.stack([gate_grad, up_grad], axis=1)[None],
            down_grad.T[None],
        )

    return local


def solution(mesh):
    both = ("dp", "ctx")
    body = make_local(mesh.shape["dp"], mesh.shape["ctx"], mesh.shape["mp"])

    return jax.shard_map(
        body,
        mesh=mesh,
        in_specs=(
            P("dp", "ctx", None),
            P("dp", None),
            P(None, both),
            P(None, both, "mp"),
            P(None, "mp", both),
            P(None, "mp", both),
            P(None, both),
            P(None, both, None, "mp"),
            P(None, "mp", both),
            P("dp", "ctx", None),
        ),
        out_specs=(
            P("dp", "ctx", None),
            P("dp", "ctx", None),
            P(None, both),
            P(None, both, "mp"),
            P(None, "mp", both),
            P(None, "mp", both),
            P(None, both),
            P(None, both, None, "mp"),
            P(None, "mp", both),
        ),
        check_vma=False,
    )
```

```python
import jax
import jax.numpy as jnp
from jax import lax
from jax.sharding import PartitionSpec as P


HEAD_DIM = 64
GROUP = 7
LANES = 128

epsilon = 1e-06
base_theta = 1000000.0


f32 = jnp.float32
bf16 = jnp.bfloat16


def rope_tables(block_locations, head_dim):
    half_dim = head_dim // 2
    inv_freq = base_theta ** (-(jnp.arange(half_dim, dtype=f32) * 2.0) / head_dim)
    angles = block_locations.astype(f32)[:, None] * inv_freq[None, :]
    angles = jnp.concatenate([angles, angles], axis=1)
    return (jnp.cos(angles), jnp.sin(angles))


def rotate(values, cosine_lookup, sine_lookup):
    half_dim = values.shape[-1] // 2
    view_shape = (values.shape[0],) + (1,) * (values.ndim - 2) + (values.shape[-1],)
    turned = jnp.concatenate([-values[..., half_dim:], values[..., :half_dim]], axis=-1)
    return values * cosine_lookup.reshape(view_shape) + turned * sine_lookup.reshape(view_shape)


def rms_forward(hidden, gain_vec):
    scale_rows = lax.rsqrt(jnp.mean(hidden * hidden, axis=-1, keepdims=True) + epsilon)
    normed = hidden * scale_rows
    return (normed, scale_rows, (normed * gain_vec.astype(f32)).astype(bf16))


def rms_backward(grad_out, normed, scale_rows, gain_vec):
    gain_grad = jnp.sum(grad_out * normed, axis=0)
    grad_normed = grad_out * gain_vec.astype(f32)
    grad_in = scale_rows * (
        grad_normed - normed * jnp.mean(grad_normed * normed, axis=-1, keepdims=True)
    )
    return (grad_in, gain_grad)


def after(value, *others):
    return lax.optimization_barrier((value,) + others)[0]


def summed(terms):
    if len(terms) == 1:
        return terms[0]
    return sum(m.astype(f32) for m in terms).astype(bf16)


def dot_nt(a, b):
    return lax.dot_general(a, b, (((1,), (1,)), ((), ())), preferred_element_type=f32)


def dot_tn(a, b):
    return lax.dot_general(a, b, (((0,), (0,)), ((), ())), preferred_element_type=f32)


def dot_nn(a, b):
    return jnp.dot(a, b, preferred_element_type=f32)


def make_local(n_dp, n_ctx, n_mp):
    n_lo = 2
    n_hi = n_ctx // n_lo
    assert n_dp == 2 and n_mp == 2 and n_hi * n_lo == n_ctx
    pair = [(0, 1), (1, 0)]
    lo_pair = [(i, i ^ 1) for i in range(n_ctx)]

    def swap_dp(v):
        return lax.ppermute(v, "dp", pair)

    def swap_mp(v):
        return lax.ppermute(v, "mp", pair)

    def swap_lo(v):
        return lax.ppermute(v, "ctx", lo_pair)

    def swap_hi(v, mask):
        perm = [(h * n_lo + e, (h ^ mask) * n_lo + e) for h in range(n_hi) for e in range(n_lo)]
        return lax.ppermute(v, "ctx", perm)

    def exchange(v, axes):
        return lax.all_to_all(v, axes, 0, 0, tiled=True)

    def in_order(flag, own, other, axis=0):
        first = flag == 0
        return jnp.stack([jnp.where(first, own, other), jnp.where(first, other, own)], axis=axis)

    def flipped(flag, pairs):
        return jnp.where(flag == 0, pairs, pairs[:, ::-1])

    def pick(flag, two):
        first = flag == 0
        return jnp.where(first, two[0], two[1]), jnp.where(first, two[1], two[0])

    def by_mask(got, hi):
        got = jnp.stack(got)
        return jnp.stack(
            [
                lax.dynamic_index_in_dim(got, jnp.bitwise_xor(hi, j), 0, keepdims=False)
                for j in range(n_hi)
            ]
        )

    def relay_masks():
        masks, step = [], n_hi // 2
        while step:
            masks.append(step)
            step //= 2
        return masks

    def scatter_hi(parts, hi):
        total = lax.dynamic_index_in_dim(parts, hi, 0, keepdims=False).astype(f32)
        for k in range(1, n_hi):
            part = lax.dynamic_index_in_dim(parts, jnp.bitwise_xor(hi, k), 0, keepdims=False)
            part = swap_hi(part, k)
            total = total + part.astype(f32)
        return total

    def gather_rows(block, c, hi, lo, start=None):
        got = [block] + [swap_hi(block, k) for k in range(1, n_hi)]
        if start is not None:
            got = [after(g, start) for g in got]
        mine = by_mask(got, hi)
        both = in_order(lo, mine, swap_lo(mine), axis=1)
        return in_order(c, both, swap_dp(both))

    def scatter_near(parts, c, lo):
        keep, sent = pick(c, parts.astype(bf16))
        keep = keep.astype(f32) + swap_dp(sent).astype(f32)
        keep, send = pick(lo, (keep[:, 0], keep[:, 1]))
        sent = send.astype(bf16)
        near = keep + swap_lo(sent).astype(f32)
        return near.astype(bf16), sent

    def gather_tokens(block):
        both = jnp.concatenate([block, swap_lo(block)], axis=0)
        return jnp.concatenate([both, swap_dp(both)], axis=0)

    def scatter_tokens(parts):
        half = parts.shape[0] // 2
        keep = parts[:half] + swap_dp(parts[half:].astype(bf16)).astype(f32)
        half = half // 2
        keep = keep[:half] + swap_lo(keep[half:].astype(bf16)).astype(f32)
        sent = keep.astype(bf16)
        return sum_mp(sent), sent

    def sum_mp(part):
        part = part.astype(bf16)
        return part.astype(f32) + swap_mp(part).astype(f32)

    def local(
        inputs,
        positions,
        attn_gain,
        qkv_weight,
        qkv_bias,
        out_weight,
        ffn_gain,
        gate_up_weight,
        down_weight,
        cotangent,
    ):
        c = lax.axis_index("dp")
        ctx = lax.axis_index("ctx")
        hi, lo = ctx // n_lo, ctx % n_lo
        tokens = inputs.shape[1]
        model_width = inputs.shape[2]
        head_dim = HEAD_DIM
        group_size = GROUP
        score_scale = head_dim ** (-0.5)
        rows = qkv_weight.shape[1]
        units = down_weight.shape[1]
        splits = n_dp * n_lo
        piece = -(-units // (splits * LANES)) * LANES
        n_shards = n_dp * n_ctx

        seq_pos = positions[0]
        my_pos = lax.dynamic_slice_in_dim(seq_pos, ctx * tokens, tokens)
        hidden = inputs[0]

        w_q = qkv_weight[0]
        width_q = w_q.shape[1]
        gain_cols = -(-rows // LANES) * LANES
        bias_cols = qkv_bias.shape[2]
        extra = jnp.concatenate(
            [
                jnp.pad(attn_gain[0], (0, gain_cols - rows)),
                jnp.pad(ffn_gain[0], (0, gain_cols - rows)),
                jnp.pad(qkv_bias[0, 0], (0, width_q - 2 * gain_cols - bias_cols)),
            ]
        )[None]
        extra = jnp.pad(extra, ((0, 7), (0, 0)))
        block_q = jnp.concatenate([w_q, extra], axis=0)
        got_q = gather_rows(block_q, c, hi, lo).reshape(n_shards, rows + 8, width_q)
        w_qkv = got_q[:, :rows].reshape(model_width, width_q)
        side = got_q[:, rows]
        gain_attn = side[:, :rows].reshape(model_width)
        gain_ffn = side[:, gain_cols : gain_cols + rows].reshape(model_width)
        b_qkv = side[:, 2 * gain_cols : 2 * gain_cols + bias_cols].reshape(width_q)

        gate_up_weight, down_weight, cotangent, my_pos, hidden, all_pos = (
            lax.optimization_barrier(
                (gate_up_weight, down_weight, cotangent, my_pos, hidden, seq_pos, block_q)
            )[:6]
        )
        shards = [gate_up_weight[0, :, 0], gate_up_weight[0, :, 1], down_weight[0].T]
        shards = [jnp.pad(s, ((0, 0), (0, splits * piece - units))) for s in shards]
        groups = [
            jnp.concatenate([s[:, q * piece : (q + 1) * piece] for s in shards], axis=1)
            for q in range(splits)
        ]
        halves = [jnp.stack(groups[e * n_dp : (e + 1) * n_dp]) for e in range(n_lo)]
        keep, send = pick(lo, halves)
        cosine_lookup, sine_lookup = rope_tables(my_pos, head_dim)
        key_pos = flipped(lo, all_pos.reshape(n_hi, n_lo, tokens))
        step = n_hi // 2
        while step:
            key_pos = flipped(hi // step % 2, key_pos.reshape(-1, 2, step * n_lo * tokens))
            step //= 2
        key_pos = key_pos.reshape(n_hi, n_lo, tokens).swapaxes(0, 1).reshape(-1)
        row_pos = jnp.tile(my_pos, group_size)
        both = in_order(lo, keep, swap_lo(send))
        block_o = after(out_weight[0].T, block_q)
        grad_out = cotangent[0]
        keep, send = pick(c, (both[:, 0], both[:, 1]))
        plane = in_order(c, keep, swap_dp(send))

        normed_a, scale_a, attn_in = rms_forward(hidden, gain_attn)
        attn_in = lax.optimization_barrier(attn_in)
        qkv_proj = dot_nn(attn_in, w_qkv) + b_qkv.astype(f32)
        qkv_proj = qkv_proj.reshape(tokens, group_size + 2, head_dim)
        query_heads = rotate(qkv_proj[:, :group_size], cosine_lookup, sine_lookup).astype(bf16)
        key_head = rotate(
            qkv_proj[:, group_size : group_size + 1], cosine_lookup, sine_lookup
        )[:, 0].astype(bf16)
        value_head = qkv_proj[:, group_size + 1].astype(bf16)
        query_rows = jnp.transpose(query_heads, (1, 0, 2)).reshape(group_size * tokens, head_dim)
        pair_kv = jnp.concatenate([key_head, value_head], axis=1)
        grad_half = gather_tokens(after(grad_out.astype(bf16), pair_kv))
        w_ot = gather_rows(block_o, c, hi, lo, pair_kv).reshape(model_width, -1)
        cut = 2 * piece
        relays = {}
        for part, block in (("gu", plane[..., :cut]), ("d", plane[..., cut:])):
            got = {0: block}
            for mask in relay_masks():
                for k in list(got):
                    got[k ^ mask] = swap_hi(got[k], mask)
            relays[part] = [got[k] for k in range(n_hi)]

        def assembled(got):
            return jnp.transpose(by_mask(got, hi), (1, 0, 2, 3, 4)).reshape(model_width, -1)

        w_gu = assembled(relays["gu"])
        pair_kv = jnp.concatenate([pair_kv] + [swap_hi(pair_kv, k) for k in range(1, n_hi)], axis=0)
        pair_kv = jnp.concatenate([pair_kv, swap_lo(pair_kv)], axis=0)
        key_all, value_all = pair_kv[:, :head_dim], pair_kv[:, head_dim:]
        allowed = key_pos[None, :] <= row_pos[:, None]
        scores = dot_nt(query_rows, key_all) * score_scale
        scores = jnp.where(allowed, scores, -1e30)
        row_max = jnp.max(scores, axis=1)
        weights_now = jnp.where(allowed, jnp.exp(scores - row_max[:, None]), 0.0)
        row_total = jnp.sum(weights_now, axis=1)
        row_accum = jnp.dot(
            weights_now,
            value_all.astype(f32),
            precision=lax.Precision.HIGHEST,
            preferred_element_type=f32,
        )
        log_total = row_max + jnp.log(row_total)
        attn_rows = (row_accum / row_total[:, None]).astype(bf16)
        attn_flat = jnp.transpose(
            attn_rows.reshape(group_size, tokens, head_dim), (1, 0, 2)
        ).reshape(tokens, group_size * head_dim)
        hidden_mid = hidden + sum_mp(dot_nt(attn_flat, w_ot))

        normed_f, scale_f, ffn_in = rms_forward(hidden_mid, gain_ffn)
        ffn_all = gather_tokens(ffn_in)
        gate_up_pre = dot_nn(ffn_all, w_gu)
        w_dt = assembled([after(v, gate_up_pre) for v in relays["d"]])
        gate_pre, up_pre = gate_up_pre[:, :piece], gate_up_pre[:, piece:]
        grad_mixed = dot_nn(grad_half, w_dt)
        sigmoid_gate = jax.nn.sigmoid(gate_pre)
        silu_gate = gate_pre * sigmoid_gate
        mixed_units = (silu_gate * up_pre).astype(bf16)
        grad_up = grad_mixed * silu_gate
        grad_gate = grad_mixed * up_pre * (sigmoid_gate + silu_gate * (1.0 - sigmoid_gate))
        grad_pre = jnp.concatenate([grad_gate, grad_up], axis=1).astype(bf16)
        ffn_in_grad, db_sent = scatter_tokens(dot_nt(grad_pre, w_gu))
        far = n_hi // 2
        own_sum, far_sum = {}, {}
        for part in ("gu", "d"):
            if part == "gu":
                full = dot_tn(ffn_all, grad_pre)
            else:
                mixed_units = after(mixed_units, own_sum["gu"][0])
                full = dot_tn(grad_half, mixed_units)
            full = full.astype(bf16).reshape(n_dp, n_hi, n_lo, rows, -1)
            full = jnp.transpose(full, (1, 0, 2, 3, 4))
            sums = {
                k: [lax.dynamic_index_in_dim(full, jnp.bitwise_xor(hi, k), 0, keepdims=False)]
                for k in range(n_hi)
            }
            for mask in reversed(relay_masks()[1:]):
                for k in sorted(sums, reverse=True):
                    if k & mask:
                        arrived = swap_hi(summed(sums.pop(k)), mask)
                        sums[k ^ mask].append(arrived)
            own_sum[part], far_sum[part] = sums[0], sums[far]
        ffn_part = dot_nt(after(mixed_units, db_sent), w_dt)
        hidden_next = hidden_mid + scatter_tokens(ffn_part)[0]
        far_sum["gu"] = [after(m, db_sent) for m in far_sum["gu"]]
        far_sum["gu"] = swap_hi(summed(far_sum["gu"]), far)

        back_ffn, gain_ffn_part = rms_backward(ffn_in_grad, normed_f, scale_f, gain_ffn)
        grad_mid = grad_out + back_ffn
        grad_mid_half = grad_mid.astype(bf16)
        grad_attn = dot_nn(grad_mid_half, w_ot).astype(bf16)
        out_part = dot_tn(grad_mid_half, attn_flat)
        out_near, _ = scatter_near(out_part.reshape(n_dp, n_hi, n_lo, rows, -1), c, lo)
        grad_rows = jnp.transpose(
            grad_attn.reshape(tokens, group_size, head_dim), (1, 0, 2)
        ).reshape(group_size * tokens, head_dim)
        delta_rows = jnp.sum(grad_rows.astype(f32) * attn_rows.astype(f32), axis=1)
        probs = jnp.where(allowed, jnp.exp(scores - log_total[:, None]), 0.0)
        grad_probs = dot_nt(grad_rows, value_all)
        grad_scores = (probs * (grad_probs - delta_rows[:, None])).astype(bf16)
        query_grad = dot_nn(grad_scores, key_all) * score_scale
        scaled = (query_rows.astype(f32) * score_scale).astype(bf16)
        kv_grad = dot_tn(grad_scores, jnp.pad(scaled, ((0, 0), (0, head_dim)))) + dot_tn(
            probs.astype(bf16), jnp.pad(grad_rows, ((0, 0), (head_dim, 0)))
        )
        far_sum["d"] = [after(m, kv_grad) for m in far_sum["d"]]
        far_sum["d"] = swap_hi(summed(far_sum["d"]), far)
        kv_grad = kv_grad.reshape(n_lo, n_hi, tokens, 2 * head_dim)
        kv_grad = kv_grad[0] + swap_lo(kv_grad[1].astype(bf16)).astype(f32)
        arrived = [swap_hi(kv_grad[k].astype(bf16), k) for k in range(1, n_hi)]
        kv_grad = kv_grad[0] + sum(m.astype(f32) for m in arrived)
        key_grad, value_grad = kv_grad[:, :head_dim], kv_grad[:, head_dim:]
        query_grad = jnp.transpose(query_grad.reshape(group_size, tokens, head_dim), (1, 0, 2))
        query_grad = rotate(query_grad, cosine_lookup, -sine_lookup)
        key_grad = rotate(key_grad[:, None], cosine_lookup, -sine_lookup)
        grad_qkv = jnp.concatenate([query_grad, key_grad, value_grad[:, None]], axis=1).reshape(
            tokens, (group_size + 2) * head_dim
        )
        bias_part = jnp.sum(grad_qkv, axis=0)
        grad_qkv_half = grad_qkv.astype(bf16)
        attn_in_grad = sum_mp(dot_nt(grad_qkv_half, w_qkv))
        back_attn, gain_attn_part = rms_backward(attn_in_grad, normed_a, scale_a, gain_attn)
        input_grad = grad_mid + back_attn
        qkv_part = dot_tn(attn_in, grad_qkv_half)

        qkv_near, qkv_sent = scatter_near(qkv_part.reshape(n_dp, n_hi, n_lo, rows, -1), c, lo)
        row_sums = scatter_hi(jnp.concatenate([qkv_near, out_near], axis=-1), hi)
        qkv_sum, out_grad = row_sums[:, :width_q], row_sums[:, width_q:]
        side = jnp.stack(
            [
                jnp.pad(v.reshape(n_shards, -1), ((0, 0), (0, gain_cols - v.shape[0] // n_shards)))
                for v in (after(v, qkv_sent) for v in (gain_attn_part, gain_ffn_part, bias_part))
            ],
            axis=1,
        )
        side = jnp.pad(side, ((0, 0), (0, 5), (0, 0)))
        side = jnp.sum(after(exchange(side, ("dp", "ctx")), row_sums), axis=0)
        by_q = {}
        for part, tie in (("gu", qkv_near), ("d", qkv_near)):
            terms = own_sum[part] + [far_sum[part]]
            w_grad = sum(after(m, tie).astype(f32) for m in terms).astype(bf16)
            keep, send = pick(c, w_grad)
            by_c = in_order(c, keep, swap_dp(send))
            keep, send = pick(lo, (by_c[:, 0], by_c[:, 1]))
            whole = in_order(lo, keep, swap_lo(send))
            by_q[part] = whole.reshape(splits, rows, -1).astype(f32)

        def units_of(part, e):
            cols = [by_q[part][q, :, e * piece : (e + 1) * piece] for q in range(splits)]
            return jnp.concatenate(cols, axis=1)[:, :units]

        gate_grad, up_grad, down_grad = units_of("gu", 0), units_of("gu", 1), units_of("d", 0)
        return (
            hidden_next[None],
            input_grad[None],
            side[:1, :rows],
            qkv_sum[None],
            side[2:3, :bias_cols][None],
            out_grad.T[None],
            side[1:2, :rows],
            jnp.stack([gate_grad, up_grad], axis=1)[None],
            down_grad.T[None],
        )

    return local


def solution(mesh):
    both = ("dp", "ctx")
    body = make_local(mesh.shape["dp"], mesh.shape["ctx"], mesh.shape["mp"])

    return jax.shard_map(
        body,
        mesh=mesh,
        in_specs=(
            P("dp", "ctx", None),
            P("dp", None),
            P(None, both),
            P(None, both, "mp"),
            P(None, "mp", both),
            P(None, "mp", both),
            P(None, both),
            P(None, both, None, "mp"),
            P(None, "mp", both),
            P("dp", "ctx", None),
        ),
        out_specs=(
            P("dp", "ctx", None),
            P("dp", "ctx", None),
            P(None, both),
            P(None, both, "mp"),
            P(None, "mp", both),
            P(None, "mp", both),
            P(None, both),
            P(None, both, None, "mp"),
            P(None, "mp", both),
        ),
        check_vma=False,
    )
```
